128 devices in a mesh: prow: 8 (over x, core), pcol: 16 (over z, y).
Axes of the slice: x: 4, y: 4, z: 4, core: 2. Of those that a mesh axis runs over, the one named last changes fastest.
Arguments:
- child_u: bfloat16 [2, 5, 8, 2, 16, 512, 128], P(None, None, 'prow', None, 'pcol'), may hold values from -5 to 5
- child_v: bfloat16 [2, 5, 8, 2, 16, 512, 128], P(None, None, 'prow', None, 'pcol'), may hold values from -5 to 5
- child_rank: int32 [2, 5, 8, 2, 16], P(None, None, 'prow', None, 'pcol'), may hold values from 0 to 128, as said below
- diag_shift: float32 [32, 512], replicated, may hold values from 0.5 to 4
Outputs:
- front_out: float32 [5, 8, 512, 2, 16, 512], P(None, 'prow', None, None, 'pcol')
The draws below stay inside these ranges and needn't reach their ends.
Inputs may be any that keep to these rules, and one draw needn't show every extreme that they name: `child_rank`: 0 on and above the block diagonal (i <= j); below it 0 where the child has no tile, else from 16 to 128.
All inputs are finite; a program needn't handle non-finite values.
Results may differ from the reference program's by a relative error of at most 0.0003.
Values may be sent and summed in bfloat16 or wider, within the bound.
No kernel may reach another device: no remote copies, remote signals or barrier semaphores. Data moves between devices by JAX's collectives and lax.ppermute only.
A program may use at most 320 MiB of HBM per device.

```python
import math
import jax
import jax.numpy as jnp
from jax import lax

BLOCK = 512
RANK_MAX = 128
CHILDREN = 2
PANELS = 2
NBLK = 40
SLAB = 32
N_PROW = 8
N_PCOL = 16


def draw_child_rank(key, part):
    key_rank = jax.random.fold_in(key, 11)
    key_keep = jax.random.fold_in(key, 23)
    shape = (CHILDREN, NBLK // N_PROW, N_PROW, SLAB // N_PCOL, N_PCOL)
    block_rows = lax.broadcasted_iota(jnp.int32, shape, 1) * N_PROW + lax.broadcasted_iota(jnp.int32, shape, 2)
    block_cols = lax.broadcasted_iota(jnp.int32, shape, 3) * N_PCOL + lax.broadcasted_iota(jnp.int32, shape, 4)
    ranks = jax.random.randint(key_rank, shape, RANK_MAX // 8, RANK_MAX + 1)
    present = jax.random.randint(key_keep, shape, 0, 4) > 0
    return jnp.where((block_rows > block_cols) & present, ranks, 0).astype(jnp.int32)


def block_levels(key, dims, split, smallest, top_value):
    loudness, own = 1.0, jax.random.fold_in(key, 6)
    for position, blocks in split:
        steps = jnp.exp(jax.random.uniform(jax.random.fold_in(own, position), (blocks,), jnp.float32, smallest / len(split), top_value / len(split)))
        loudness = loudness * jnp.repeat(steps, dims[position] // blocks).reshape([-1 if axis == position else 1 for axis in range(len(dims))])
    return loudness


def scatter_about(key, shape, deviation, limit, pieces=(), kind=jnp.bfloat16):
    array = deviation * jax.random.normal(key, shape, jnp.float32)
    if pieces:
        array = array * block_levels(key, shape, pieces, -0.22, 0.18)
    return jnp.clip(array, -limit, limit).astype(kind)


def setup_inputs(seed: int = 0) -> dict:
    splits = jax.random.split(jax.random.key(seed), 5)
    child_u = scatter_about(splits[0], (CHILDREN, NBLK // N_PROW, N_PROW, SLAB // N_PCOL, N_PCOL, BLOCK, RANK_MAX), 0.35, 5.0, ((2, 8), (4, 16)))
    child_v = scatter_about(splits[1], (CHILDREN, NBLK // N_PROW, N_PROW, SLAB // N_PCOL, N_PCOL, BLOCK, RANK_MAX), 0.35, 5.0, ((2, 8), (4, 16)))
    child_rank = draw_child_rank(jax.random.fold_in(splits[4], 71), 0)
    diag_shift = jnp.clip(jnp.exp(jax.random.uniform(splits[3], (SLAB, BLOCK), jnp.float32, math.log(0.5), math.log(4.0))), 0.5, 4.0)
    return {"child_u": child_u, "child_v": child_v, "child_rank": child_rank, "diag_shift": diag_shift}


def reference(child_u, child_v, child_rank, diag_shift):
    precise = lax.Precision.HIGHEST
    rank_grid = child_rank.reshape(CHILDREN, NBLK, SLAB)
    keep_mask = (jnp.arange(RANK_MAX, dtype=jnp.int32)[None, None, None, :] < rank_grid[:, :, :, None]).astype(jnp.bfloat16)
    left_factor = child_u.reshape(CHILDREN, NBLK, SLAB, BLOCK, RANK_MAX) * keep_mask[:, :, :, None, :]
    right_factor = child_v.reshape(CHILDREN, NBLK, SLAB, BLOCK, RANK_MAX) * keep_mask[:, :, :, None, :]
    left_cols = left_factor.transpose(2, 0, 1, 3, 4)
    right_cols = right_factor.transpose(2, 0, 1, 3, 4)

    def assemble(operands):
        left_part = operands[0].astype(jnp.float32)
        right_part = operands[1].astype(jnp.float32)
        tile_col = jnp.einsum('ciak,cibk->iab', left_part, right_part, precision=precise)
        column_sum = jnp.einsum('ciak,cibk->ab', right_part, right_part, precision=precise)
        return (tile_col, column_sum)
    front_cols, column_sums = lax.map(assemble, (left_cols, right_cols))

    def row_part(row_factor):
        row_factor = row_factor.astype(jnp.float32)
        return jnp.einsum('cjak,cjbk->ab', row_factor, row_factor, precision=precise)
    row_sums = lax.map(row_part, left_factor.transpose(1, 0, 2, 3, 4)[:SLAB])
    diagonal_index = jnp.arange(SLAB, dtype=jnp.int32)
    identity = jnp.eye(BLOCK, dtype=jnp.float32)
    diag_terms = row_sums + column_sums + identity[None] * diag_shift[:, None, :]
    front_cols = front_cols.at[diagonal_index, diagonal_index].add(diag_terms)
    block_rows = jnp.arange(NBLK, dtype=jnp.int32)
    panel_list = []
    for panel_index in range(PANELS):
        factor = jnp.linalg.cholesky(front_cols[panel_index, panel_index])
        solved = lax.linalg.triangular_solve(factor, front_cols[panel_index].reshape(NBLK * BLOCK, BLOCK), left_side=False, lower=True, transpose_a=True).reshape(NBLK, BLOCK, BLOCK)
        below_mask = (block_rows > panel_index)[:, None, None]
        solved = jnp.where(below_mask, solved, 0.0)
        pivot_diag = jnp.diagonal(factor)
        at_pivot = (block_rows == panel_index)[:, None, None]
        panel_list.append(jnp.where(at_pivot, (factor * pivot_diag[None, :])[None], solved * pivot_diag[None, None, :]))
        rounded = lax.optimization_barrier(solved.astype(jnp.bfloat16)).astype(jnp.float32)

        def update(operands, rounded=rounded):
            return operands[0] - jnp.einsum('iab,cb->iac', rounded, operands[1], precision=precise)
        front_cols = lax.map(update, (front_cols, rounded[:SLAB]))
    slab_index = jnp.arange(SLAB, dtype=jnp.int32)
    lower_mask = (block_rows[None, :] >= slab_index[:, None])[:, :, None, None]
    final = jnp.where(lower_mask, front_cols, 0.0)
    final = final.at[:PANELS].set(jnp.stack(panel_list))
    final = final.reshape(SLAB // N_PCOL, N_PCOL, NBLK // N_PROW, N_PROW, BLOCK, BLOCK).transpose(2, 3, 4, 0, 1, 5)
    return final
```

```python
import functools
import jax
import jax.numpy as jnp
from jax import lax
from jax.experimental import pallas as pl
from jax.experimental.pallas import tpu as pltpu
from jax.sharding import PartitionSpec as P

F32 = jnp.float32
BF16 = jnp.bfloat16
PROW, PCOL = 8, 16
ROWS, COLS, KIDS = 5, 2, 2
N, RK = 512, 128
TRI = [(a, b) for a in range(4) for b in range(a + 1)]
PACK = 128 * len(TRI)
KSLAB = PACK // PROW
RSLAB = PACK // PCOL
VMEM = pl.BlockSpec(memory_space=pltpu.VMEM)
SMEM = pl.BlockSpec(memory_space=pltpu.SMEM)
EXACT = lax.Precision.HIGHEST


def shape(dims, dtype):
    return jax.ShapeDtypeStruct(dims, dtype)


def params(mib):
    return pltpu.CompilerParams(vmem_limit_bytes=mib << 20)


def nt(a, b, precision=None):
    return lax.dot_general(
        a, b, (((1,), (1,)), ((), ())), precision=precision, preferred_element_type=F32
    )


def nn(a, b, precision=None):
    return lax.dot_general(
        a, b, (((1,), (0,)), ((), ())), precision=precision, preferred_element_type=F32
    )


def halves(x):
    hi = x.astype(BF16)
    return hi, (x - hi.astype(F32)).astype(BF16)


def kept(tile, rank):
    lane = lax.broadcasted_iota(jnp.int32, tile.shape, 1)
    return jnp.where(lane < rank, tile, jnp.zeros_like(tile))


def column_kernel(rank, meta, v, *refs):
    out, (cat, packed) = refs[:PROW], refs[PROW:]
    own = meta[0]
    for t in range(COLS):
        for c in range(KIDS):
            for r in range(ROWS):
                at = (c * ROWS + r) * RK
                cat[:, at : at + RK] = kept(v[c, r, t], rank[c, r, t])
        total = nt(cat[...], cat[...])
        for n, (a, b) in enumerate(TRI):
            packed[128 * n : 128 * n + 128, :] = total[
                128 * a : 128 * a + 128, 128 * b : 128 * b + 128
            ]
        for s in range(PROW):
            slab = lax.rem(own + s, PROW)
            out[s][t] = packed[pl.ds(pl.multiple_of(slab * KSLAB, 8), KSLAB), :]


def pieces_kernel(rank, meta, u, v, *refs):
    raw, tile, cols, rsum, cat, masked = (
        refs[:16],
        refs[16:24],
        refs[24:40],
        refs[40],
        refs[41],
        refs[42],
    )
    root = jnp.where(meta[1] == 1, 1, 0)
    for c in range(KIDS):
        for r in range(ROWS):
            masked[c * ROWS + r] = kept(u[c, r, 0], rank[c, r, 0])
            masked[(KIDS + c) * ROWS + r] = kept(v[c, r, 0], rank[c, r, 0])
    for s in range(16):
        raw[s][...] = masked[:, 32 * s : 32 * s + 32, :]
    for s in range(8):
        for a in range(2 * KIDS):
            tile[s][a] = masked[a * ROWS, 64 * s : 64 * s + 64, :]
            for h in range(2):
                row = lax.rem(root + h, 2)
                cols[2 * s + h][a] = masked[a * ROWS + row, 64 * s : 64 * s + 64, :]
                cols[2 * s + h][4 + a] = masked[
                    a * ROWS + 2 + row, 64 * s : 64 * s + 64, :
                ]
    for r in range(4):
        for c in range(KIDS):
            cat[:, 2 * c * RK : (2 * c + 1) * RK] = masked[c * ROWS + r]
            cat[:, (2 * c + 1) * RK : (2 * c + 2) * RK] = kept(u[c, r, 1], rank[c, r, 1])
        total = nt(cat[...], cat[...])
        for n, (a, b) in enumerate(TRI):
            for e in range(128 // 16):
                line = 128 * n + 16 * e
                rsum[line // RSLAB, r, line % RSLAB : line % RSLAB + 16, :] = total[
                    128 * a + 16 * e : 128 * a + 16 * e + 16, 128 * b : 128 * b + 128
                ]


def base_inverse(block):
    lane = lax.broadcasted_iota(jnp.int32, (8, 128), 1)
    sub = lax.broadcasted_iota(jnp.int32, (8, 128), 0)
    rows = [block[8 * v : 8 * v + 8, :] for v in range(16)]

    def wide(x):
        return jnp.broadcast_to(x, (8, 128))

    for J in range(16):
        inside = (lane >= 8 * J) & (lane < 8 * J + 8)
        B = [wide(rows[J][:, 8 * J + n : 8 * J + n + 1]) for n in range(8)]
        fwd = jnp.where(inside, jnp.where(lane - 8 * J == sub, 1.0, 0.0), rows[J])
        full = fwd
        roots = jnp.zeros((8, 128), F32)
        for k in range(8):
            r = lax.rsqrt(wide(B[k][k : k + 1, :]))
            row = wide(full[k : k + 1, :])
            mult = jnp.where(sub == k, 0.0, B[k] * (r * r))
            full = full - mult * row
            fwd = fwd - jnp.where(sub > k, mult, 0.0) * row
            for n in range(k + 1, 8):
                B[n] = B[n] - mult * wide(B[n][k : k + 1, :])
            roots = jnp.where(sub == k, r, roots)
        rows[J] = fwd * roots
        scaled = full * (roots * roots)
        Y = [wide(scaled[n : n + 1, :]) for n in range(8)]
        for v in range(J + 1, 16):
            b = [wide(rows[v][:, 8 * J + n : 8 * J + n + 1]) * Y[n] for n in range(8)]
            t = ((b[0] + b[1]) + (b[2] + b[3])) + ((b[4] + b[5]) + (b[6] + b[7]))
            rows[v] = jnp.where(inside, 0.0, rows[v]) - t
    return jnp.concatenate(
        [jnp.where(lane <= sub + 8 * v, rows[v], 0.0) for v in range(16)], axis=0
    )


def factor(A, C, M):
    i = lax.broadcasted_iota(jnp.int32, (128, 128), 0)
    j = lax.broadcasted_iota(jnp.int32, (128, 128), 1)
    M[...] = jnp.zeros_like(M)
    C[...] = jnp.zeros_like(C)
    for b in range(4):
        at = slice(128 * b, 128 * b + 128)
        inv = base_inverse(A[at, at])
        if b:
            left = nn(C[at, 0 : 128 * b], M[0 : 128 * b, 0 : 128 * b], EXACT)
            M[at, 0 : 128 * b] = -nn(inv, left, EXACT)
        M[at, at] = inv
        C[at, at] = jnp.where(i >= j, nt(A[at, at], inv, EXACT), 0.0)
        if b < 3:
            below = slice(128 * b + 128, N)
            panel = nt(A[below, at], inv, EXACT)
            C[below, at] = panel
            A[below, below] = A[below, below] - nt(panel, panel, EXACT)


def add_shift(A, line):
    i = lax.broadcasted_iota(jnp.int32, (N, N), 0)
    j = lax.broadcasted_iota(jnp.int32, (N, N), 1)
    A[...] = A[...] + jnp.where(i == j, line, 0.0)


def unpack(A, packed, mirror):
    for n, (a, b) in enumerate(TRI):
        block = packed[128 * n : 128 * n + 128, :]
        A[128 * a : 128 * a + 128, 128 * b : 128 * b + 128] = block
        if a != b:
            A[128 * b : 128 * b + 128, 128 * a : 128 * a + 128] = (
                block.T if mirror else jnp.zeros_like(block)
            )


def first_kernel(
    meta, own, other, town, tother, shift, C, Mh, Ml, Gb, A1, packed, tile, A, M
):
    x, core = meta[2], meta[3]
    for s in range(4):
        chip = lax.rem(x - s + 4, 4)
        for part, tpart, lane in ((own, town, core), (other, tother, 1 - core)):
            place = 2 * chip + lane
            for k in range(2):
                packed[k, pl.ds(pl.multiple_of(place * KSLAB, 8), KSLAB), :] = part[s, k]
            for a in range(4):
                tile[a, pl.ds(pl.multiple_of(place * 64, 16), 64), :] = tpart[s, a]
    unpack(A, packed.at[0], False)
    add_shift(A, shift[0:1, :])
    factor(A, C, M)
    hi, lo = halves(M[...])
    Mh[...] = hi
    Ml[...] = lo
    U = jnp.concatenate([tile[0], tile[1]], axis=1)
    V = jnp.concatenate([tile[2], tile[3]], axis=1)
    wh, wl = halves(nn(hi, V) + nn(lo, V))
    G = (nt(U, wh) + nt(U, wl)).astype(BF16)
    Gb[...] = G
    unpack(A, packed.at[1], False)
    add_shift(A, shift[1:2, :])
    A1[...] = A[...] + (nt(U, U) - nt(G, G))


def second_kernel(A1, Gb, C, Mh, Ml, Xh, Xl, A, M):
    A[...] = A1[...]
    factor(A, C, M)
    hi, lo = halves(M[...])
    Mh[...] = hi
    Ml[...] = lo
    xh, xl = halves(nn(hi, Gb[...]) + nn(lo, Gb[...]))
    Xh[...] = xh
    Xl[...] = xl


def final_kernel(
    rank, meta, shift, u, v, rb, rc, rsum, ksum,
    C0, M0h, M0l, C1, M1h, M1l, X1h, X1l, out, gcol, packed, D
):
    r = pl.program_id(0)
    p, q = meta[0], meta[1]
    home = lax.rem(q, PROW)

    def solve(i, U0, V0, U1, V1):
        wh, wl = halves(nn(M0h[...], V0) + nn(M0l[...], V0))
        G0 = nt(U0, wh) + nt(U0, wl)
        G0 = jnp.where(i > 0, G0, 0.0)
        b0 = G0.astype(BF16)
        wh, wl = halves(nn(M1h[...], V1) + nn(M1l[...], V1))
        G1 = (nt(U1, wh) + nt(U1, wl)) - (nt(b0, X1h[...]) + nt(b0, X1l[...]))
        G1 = jnp.where(i > 1, G1, 0.0)
        return G0, G1, b0, G1.astype(BF16)

    def pair(get, first):
        return jnp.concatenate([get(first), get(first + 1)], axis=1)

    @pl.when(r == 0)
    def _():
        for t in range(COLS):
            parts = []
            for k in range(2):
                def get(a, k=k, t=t):
                    return jnp.concatenate(
                        [rc[lax.rem(home + s, PROW), k, 4 * t + a] for s in range(8)],
                        axis=0,
                    )
                parts += [pair(get, 0), pair(get, 2)]
            _, _, b0, b1 = solve(q + PCOL * t, *parts)
            gcol[t, :, 0:N] = b0
            gcol[t, :, N : 2 * N] = b1

    i = r * PROW + p
    parts = []
    for k in range(2):
        def get(a, k=k):
            whole = rb[:, k, a * ROWS + r]
            if k:
                whole = jnp.concatenate([whole[1:], whole[:1]], axis=0)
            return whole.reshape(N, RK)
        parts += [pair(get, 0), pair(get, 2)]
    G0, G1, b0, b1 = solve(i, *parts)
    gb = jnp.concatenate([b0, b1], axis=1)

    def put(t, value):
        for b in range(4):
            out[0, :, 4 * t + b, :] = value[:, 128 * b : 128 * b + 128]

    def trailing(t):
        j = q + PCOL * t
        U = jnp.concatenate([u[c, 0, t] for c in range(KIDS)], axis=1)
        V = jnp.concatenate([kept(v[c, 0, t], rank[c, r, t]) for c in range(KIDS)], axis=1)
        acc = nt(U, V) - nt(gb, gcol[t])
        put(t, jnp.where(i >= j, acc, 0.0))

        @pl.when(i == j)
        def _():
            for e in range(PROW):
                packed[KSLAB * e : KSLAB * e + KSLAB, :] = ksum[e, t]
            for e in range(PCOL):
                at = slice(RSLAB * e, RSLAB * e + RSLAB)
                packed[at, :] = packed[at, :] + rsum[e, r]
            unpack(D, packed, True)
            add_shift(D, shift[pl.ds(j, 1), :])
            put(t, acc + D[...])

    def panel(k, C, G):
        a = lax.broadcasted_iota(jnp.int32, (N, N), 0)
        b = lax.broadcasted_iota(jnp.int32, (N, N), 1)
        pivots = jnp.sum(jnp.where(a == b, C[...], 0.0), axis=0, keepdims=True)

        @pl.when(i == k)
        def _():
            put(0, C[...] * pivots)

        @pl.when(i != k)
        def _():
            put(0, G * pivots)

    @pl.when(q > 1)
    def _():
        trailing(0)

    @pl.when(q == 0)
    def _():
        panel(0, C0, G0)

    @pl.when(q == 1)
    def _():
        panel(1, C1, G1)

    trailing(1)


def total(values):
    return functools.reduce(lambda a, b: a + b, values)


def pick(flag, value):
    return jnp.where(flag, value, jnp.zeros_like(value))


def on_device(child_u, child_v, child_rank, diag_shift):
    p = lax.axis_index("prow")
    q = lax.axis_index("pcol")
    x, core = p // 2, p % 2
    z, y = q // 4, q % 4
    both = ("prow", "pcol")
    rank = child_rank[:, :, 0, :, 0]
    u = child_u[:, :, 0, :, 0]
    v = child_v[:, :, 0, :, 0]
    meta = jnp.stack([p, q, x, core]).astype(jnp.int32)

    kout = pl.pallas_call(
        column_kernel,
        out_shape=[shape((COLS, KSLAB, 128), F32)] * PROW,
        in_specs=[SMEM, SMEM, VMEM],
        out_specs=[VMEM] * PROW,
        scratch_shapes=[
            pltpu.VMEM((N, KIDS * ROWS * RK), BF16),
            pltpu.VMEM((PACK, 128), F32),
        ],
        compiler_params=params(32),
        name="column_sums",
    )(rank, meta, v)
    parts = pl.pallas_call(
        pieces_kernel,
        out_shape=[shape((4 * ROWS, 32, RK), BF16)] * 16
        + [shape((4, 64, RK), BF16)] * 8
        + [shape((8, 64, RK), BF16)] * 16
        + [shape((PCOL, 4, RSLAB, 128), F32)],
        in_specs=[SMEM, SMEM, VMEM, VMEM],
        out_specs=[VMEM] * 41,
        scratch_shapes=[
            pltpu.VMEM((N, 4 * RK), BF16),
            pltpu.VMEM((4 * ROWS, N, RK), BF16),
        ],
        compiler_params=params(48),
        name="pieces",
    )(rank, meta, u, v)
    raw, tile, cols, rsum = parts[:16], parts[16:24], parts[24:40], parts[40]

    kslab = kout[0] + total(
        lax.ppermute(kout[s], "prow", [(i, (i + s) % 8) for i in range(8)])
        for s in range(1, 8)
    )
    tslab = pick((p == 1) & (q == 0), tile[1]) + total(
        lax.ppermute(tile[d], both, [(PCOL, PCOL * d)]) for d in range(8) if d != 1
    )
    ky = [lax.ppermute(kslab[0], "pcol", [(i, (i + s) % 4) for i in range(4)]) for s in range(1, 4)]
    ty = [lax.ppermute(tslab, "pcol", [(0, s)]) for s in range(1, 4)]
    k0 = pick(y == 0, kslab[0]) + total(pick(y == s, ky[s - 1]) for s in range(1, 4))
    k1 = pick(y == 1, kslab[0]) + total(pick((y + 3) % 4 == s, ky[s - 1]) for s in range(1, 4))
    kz = pick(z == 0, jnp.stack([k0, k1]))
    tz = pick(z == 0, tslab + total(ty))
    down = [[(i, 4 * s + i) for i in range(4)] for s in range(1, 4)]
    kz = kz + total(lax.ppermute(kz, "pcol", pairs) for pairs in down)
    tz = tz + total(lax.ppermute(tz, "pcol", pairs) for pairs in down)
    turn = [
        [(2 * a + c, 2 * ((a + s) % 4) + c) for a in range(4) for c in range(2)]
        for s in range(1, 4)
    ]
    swap = [(i, i ^ 1) for i in range(8)]
    kown = jnp.stack([kz] + [lax.ppermute(kz, "prow", pairs) for pairs in turn])
    town = jnp.stack([tz] + [lax.ppermute(tz, "prow", pairs) for pairs in turn])
    kother = lax.ppermute(kown, "prow", swap)
    tother = lax.ppermute(town, "prow", swap)

    got = [lax.ppermute(raw[s], "pcol", [(0, s), (1, (1 + s) % 16)]) for s in range(1, 16)]
    piece = jnp.stack(
        [
            pick(q == k, raw[0]) + total(pick((q + 16 - k) % 16 == s, got[s - 1]) for s in range(1, 16))
            for k in range(2)
        ]
    )
    rows_all = lax.all_gather(piece, "pcol")
    got = {}
    for s in range(8):
        for h in range(2):
            pairs = [
                (a * PCOL + k, ((a + s) % 8) * PCOL + a + 8 * (h ^ k))
                for a in range(8)
                for k in range(2)
            ]
            got[s, h] = lax.ppermute(cols[2 * s + h], both, pairs)
    step, side = (p - q % 8 + 8) % 8, q // 8
    piece = jnp.stack(
        [
            total(pick((step == s) & ((side + k) % 2 == h), got[s, h]) for s in range(8) for h in range(2))
            for k in range(2)
        ]
    )
    cols_all = lax.all_gather(piece, "prow")
    kall = lax.all_gather(kslab, "prow")
    rown = lax.psum_scatter(rsum.reshape(-1, 128), "pcol", scatter_dimension=0, tiled=True)
    rall = lax.all_gather(rown, "pcol", tiled=True).reshape(PCOL, 4, RSLAB, 128)

    C0, M0h, M0l, g01, A1 = pl.pallas_call(
        first_kernel,
        out_shape=[
            shape((N, N), F32),
            shape((N, N), BF16),
            shape((N, N), BF16),
            shape((N, N), BF16),
            shape((N, N), F32),
        ],
        in_specs=[SMEM] + [VMEM] * 5,
        out_specs=[VMEM] * 5,
        scratch_shapes=[
            pltpu.VMEM((2, PACK, 128), F32),
            pltpu.VMEM((4, N, RK), BF16),
            pltpu.VMEM((N, N), F32),
            pltpu.VMEM((N, N), F32),
        ],
        compiler_params=params(32),
        name="first_pivot",
    )(meta, kown, kother, town, tother, diag_shift)
    C1, M1h, M1l, X1h, X1l = pl.pallas_call(
        second_kernel,
        out_shape=[shape((N, N), F32)] + [shape((N, N), BF16)] * 4,
        in_specs=[VMEM] * 2,
        out_specs=[VMEM] * 5,
        scratch_shapes=[pltpu.VMEM((N, N), F32)] * 2,
        compiler_params=params(32),
        name="second_pivot",
    )(A1, g01)
    tiles = pl.BlockSpec((KIDS, 1, COLS, N, RK), lambda r: (0, r, 0, 0, 0))
    out = pl.pallas_call(
        final_kernel,
        grid=(ROWS,),
        out_shape=shape((ROWS, N, COLS * 4, 128), F32),
        in_specs=[SMEM, SMEM, VMEM, tiles, tiles] + [VMEM] * 12,
        out_specs=pl.BlockSpec((1, N, COLS * 4, 128), lambda r: (r, 0, 0, 0)),
        scratch_shapes=[
            pltpu.VMEM((COLS, N, 2 * N), BF16),
            pltpu.VMEM((PACK, 128), F32),
            pltpu.VMEM((N, N), F32),
        ],
        compiler_params=params(60),
        name="panels_and_update",
    )(rank, meta, diag_shift, u, v, rows_all, cols_all, rall, kall,
      C0, M0h, M0l, C1, M1h, M1l, X1h, X1l)
    return out.reshape(ROWS, 1, N, COLS, 1, N)


def solution(mesh):
    placed = (
        P(None, None, "prow", None, "pcol", None, None),
        P(None, None, "prow", None, "pcol", None, None),
        P(None, None, "prow", None, "pcol"),
        P(),
    )
    return jax.shard_map(
        on_device,
        mesh=mesh,
        in_specs=placed,
        out_specs=P(None, "prow", None, None, "pcol", None),
        check_vma=False,
    )
```

```python
import functools
import jax
import jax.numpy as jnp
from jax import lax
from jax.experimental import pallas as pl
from jax.experimental.pallas import tpu as pltpu
from jax.sharding import PartitionSpec as P

F32 = jnp.float32
BF16 = jnp.bfloat16
PROW, PCOL = 8, 16
ROWS, COLS, KIDS = 5, 2, 2
N, RK = 512, 128
TRI = [(a, b) for a in range(4) for b in range(a + 1)]
PACK = 128 * len(TRI)
KSLAB = PACK // PROW
RSLAB = PACK // PCOL
VMEM = pl.BlockSpec(memory_space=pltpu.VMEM)
SMEM = pl.BlockSpec(memory_space=pltpu.SMEM)
EXACT = lax.Precision.HIGHEST


def shape(dims, dtype):
    return jax.ShapeDtypeStruct(dims, dtype)


def cost(us):
    return pl.CostEstimate(flops=us * 1_000_000_000, transcendentals=0, bytes_accessed=1 << 20)


def params(mib):
    return pltpu.CompilerParams(vmem_limit_bytes=mib << 20)


def nt(a, b, precision=None):
    return lax.dot_general(
        a, b, (((1,), (1,)), ((), ())), precision=precision, preferred_element_type=F32
    )


def nn(a, b, precision=None):
    return lax.dot_general(
        a, b, (((1,), (0,)), ((), ())), precision=precision, preferred_element_type=F32
    )


def halves(x):
    hi = x.astype(BF16)
    return hi, (x - hi.astype(F32)).astype(BF16)


def kept(tile, rank):
    lane = lax.broadcasted_iota(jnp.int32, tile.shape, 1)
    return jnp.where(lane < rank, tile, jnp.zeros_like(tile))


def column_kernel(rank, v, first, second, cat):
    for t, out in enumerate((first, second)):
        for c in range(KIDS):
            for r in range(ROWS):
                at = (c * ROWS + r) * RK
                cat[:, at : at + RK] = kept(v[c, r, t], rank[c, r, t])
        total = nt(cat[...], cat[...])
        for n, (a, b) in enumerate(TRI):
            out[128 * n : 128 * n + 128, :] = total[
                128 * a : 128 * a + 128, 128 * b : 128 * b + 128
            ]


def pieces_kernel(rank, meta, u, v, *refs):
    raw, tile, cols, masked = refs[:4], refs[4], refs[5:7], refs[7]
    root = jnp.where(meta[1] == 1, 1, 0)
    for c in range(KIDS):
        for r in range(ROWS):
            masked[c * ROWS + r] = kept(u[c, r, 0], rank[c, r, 0])
            masked[(KIDS + c) * ROWS + r] = kept(v[c, r, 0], rank[c, r, 0])
    for s in range(16):
        raw[s // 4][s % 4] = masked[:, 32 * s : 32 * s + 32, :]
    for s in range(8):
        part = slice(64 * s, 64 * s + 64)
        for a in range(2 * KIDS):
            tile[s, a] = masked[a * ROWS, part, :]
            for h in range(2):
                row = lax.rem(root + h, 2)
                cols[h][s, a] = masked[a * ROWS + row, part, :]
                cols[h][s, 4 + a] = masked[a * ROWS + 2 + row, part, :]


def row_kernel(rank, u, _, rsum, cat):
    for r in range(4):
        for c in range(KIDS):
            for t in range(COLS):
                at = (2 * c + t) * RK
                cat[:, at : at + RK] = kept(u[c, r, t], rank[c, r, t])
        total = nt(cat[...], cat[...])
        for n, (a, b) in enumerate(TRI):
            for e in range(128 // 16):
                line = 128 * n + 16 * e
                rsum[line // RSLAB, r, line % RSLAB : line % RSLAB + 16, :] = total[
                    128 * a + 16 * e : 128 * a + 16 * e + 16, 128 * b : 128 * b + 128
                ]


def base_inverse(block):
    lane = lax.broadcasted_iota(jnp.int32, (8, 128), 1)
    sub = lax.broadcasted_iota(jnp.int32, (8, 128), 0)
    rows = [block[8 * v : 8 * v + 8, :] for v in range(16)]

    def wide(x):
        return jnp.broadcast_to(x, (8, 128))

    for J in range(16):
        inside = (lane >= 8 * J) & (lane < 8 * J + 8)
        B = [wide(rows[J][:, 8 * J + n : 8 * J + n + 1]) for n in range(8)]
        fwd = jnp.where(inside, jnp.where(lane - 8 * J == sub, 1.0, 0.0), rows[J])
        full = fwd
        roots = jnp.zeros((8, 128), F32)
        for k in range(8):
            r = lax.rsqrt(wide(B[k][k : k + 1, :]))
            row = wide(full[k : k + 1, :])
            mult = jnp.where(sub == k, 0.0, B[k] * (r * r))
            full = full - mult * row
            fwd = fwd - jnp.where(sub > k, mult, 0.0) * row
            for n in range(k + 1, 8):
                B[n] = B[n] - mult * wide(B[n][k : k + 1, :])
            roots = jnp.where(sub == k, r, roots)
        rows[J] = fwd * roots
        scaled = full * (roots * roots)
        Y = [wide(scaled[n : n + 1, :]) for n in range(8)]
        for v in range(J + 1, 16):
            b = [wide(rows[v][:, 8 * J + n : 8 * J + n + 1]) * Y[n] for n in range(8)]
            t = ((b[0] + b[1]) + (b[2] + b[3])) + ((b[4] + b[5]) + (b[6] + b[7]))
            rows[v] = jnp.where(inside, 0.0, rows[v]) - t
    return jnp.concatenate(
        [jnp.where(lane <= sub + 8 * v, rows[v], 0.0) for v in range(16)], axis=0
    )


def factor(A, C, M, steps):
    i = lax.broadcasted_iota(jnp.int32, (128, 128), 0)
    j = lax.broadcasted_iota(jnp.int32, (128, 128), 1)
    if steps[0] == 0:
        M[...] = jnp.zeros_like(M)
        C[...] = jnp.zeros_like(C)
    for b in steps:
        at = slice(128 * b, 128 * b + 128)
        inv = base_inverse(A[at, at])
        if b:
            left = nn(C[at, 0 : 128 * b], M[0 : 128 * b, 0 : 128 * b], EXACT)
            M[at, 0 : 128 * b] = -nn(inv, left, EXACT)
        M[at, at] = inv
        C[at, at] = jnp.where(i >= j, nt(A[at, at], inv, EXACT), 0.0)
        if b < 3:
            below = slice(128 * b + 128, N)
            panel = nt(A[below, at], inv, EXACT)
            C[below, at] = panel
            A[below, below] = A[below, below] - nt(panel, panel, EXACT)


def add_shift(A, line):
    i = lax.broadcasted_iota(jnp.int32, (N, N), 0)
    j = lax.broadcasted_iota(jnp.int32, (N, N), 1)
    A[...] = A[...] + jnp.where(i == j, line, 0.0)


def unpack(A, packed, mirror):
    for n, (a, b) in enumerate(TRI):
        block = packed[128 * n : 128 * n + 128, :]
        A[128 * a : 128 * a + 128, 128 * b : 128 * b + 128] = block
        if a != b:
            A[128 * b : 128 * b + 128, 128 * a : 128 * a + 128] = (
                block.T if mirror else jnp.zeros_like(block)
            )


def gather_kernel(meta, own, other, shift, A, C, M, K1, packed):
    x, core = meta[2], meta[3]
    for s in range(4):
        chip = lax.rem(x - s + 4, 4)
        for part, lane in ((own, core), (other, 1 - core)):
            place = 2 * chip + lane
            at = pl.ds(pl.multiple_of(place * KSLAB, 8), KSLAB)
            packed[at, :] = part[s, 0:KSLAB, :]
            K1[at, :] = part[s, KSLAB : 2 * KSLAB, :]
    unpack(A, packed, False)
    add_shift(A, shift[0:1, :])
    factor(A, C, M, (0, 1))


def take(refs, into):
    for ref, scratch in zip(refs, into):
        scratch[...] = ref[...]


def first_kernel(
    meta, A0, C0, M0, K1, town, tother, shift, C, Mh, Ml, Gb, A1, A, M, tile
):
    x, core = meta[2], meta[3]
    for s in range(4):
        chip = lax.rem(x - s + 4, 4)
        for part, lane in ((town, core), (tother, 1 - core)):
            line = pl.multiple_of((2 * chip + lane) * 64, 16)
            for a in range(4):
                tile[a, pl.ds(line, 64), :] = part[s, a]
    take((A0, C0, M0), (A, C, M))
    factor(A, C, M, (2, 3))
    hi, lo = halves(M[...])
    Mh[...] = hi
    Ml[...] = lo
    U = jnp.concatenate([tile[0], tile[1]], axis=1)
    V = jnp.concatenate([tile[2], tile[3]], axis=1)
    wh, wl = halves(nn(hi, V) + nn(lo, V))
    G = (nt(U, wh) + nt(U, wl)).astype(BF16)
    Gb[...] = G
    unpack(A, K1, False)
    add_shift(A, shift[1:2, :])
    A1[...] = A[...] + (nt(U, U) - nt(G, G))


def half_kernel(A1, A, C, M):
    A[...] = A1[...]
    factor(A, C, M, (0, 1))


def second_kernel(A1, C1, M1, Gb, C, Mh, Ml, Xh, Xl, A, M):
    take((A1, C1, M1), (A, C, M))
    factor(A, C, M, (2, 3))
    hi, lo = halves(M[...])
    Mh[...] = hi
    Ml[...] = lo
    xh, xl = halves(nn(hi, Gb[...]) + nn(lo, Gb[...]))
    Xh[...] = xh
    Xl[...] = xl


def final_kernel(
    rank, meta, shift, u, v, rb, rc, rsum, ksum,
    C0, M0h, M0l, C1, M1h, M1l, X1h, X1l, out, gcol, packed, D
):
    r = pl.program_id(0)
    p, q = meta[0], meta[1]

    def solve(i, U0, V0, U1, V1):
        wh, wl = halves(nn(M0h[...], V0) + nn(M0l[...], V0))
        G0 = nt(U0, wh) + nt(U0, wl)
        G0 = jnp.where(i > 0, G0, 0.0)
        b0 = G0.astype(BF16)
        wh, wl = halves(nn(M1h[...], V1) + nn(M1l[...], V1))
        G1 = (nt(U1, wh) + nt(U1, wl)) - (nt(b0, X1h[...]) + nt(b0, X1l[...]))
        G1 = jnp.where(i > 1, G1, 0.0)
        return G0, G1, b0, G1.astype(BF16)

    def pair(get, first):
        return jnp.concatenate([get(first), get(first + 1)], axis=1)

    @pl.when(r == 0)
    def _():
        for t in range(COLS):
            parts = []
            for k in range(2):
                def get(a, k=k, t=t):
                    return jnp.concatenate(
                        [rc[s, k, 4 * t + a] for s in range(PROW)], axis=0
                    )
                parts += [pair(get, 0), pair(get, 2)]
            _, _, b0, b1 = solve(q + PCOL * t, *parts)
            gcol[t, :, 0:N] = b0
            gcol[t, :, N : 2 * N] = b1

    i = r * PROW + p
    parts = []
    for k in range(2):
        def get(a, k=k):
            whole = rb[:, k, a * ROWS + r]
            if k:
                order = [4 * zz + yy for zz in range(4) for yy in (1, 2, 3, 0)]
                whole = jnp.concatenate([whole[e : e + 1] for e in order], axis=0)
            return whole.reshape(N, RK)
        parts += [pair(get, 0), pair(get, 2)]
    G0, G1, b0, b1 = solve(i, *parts)
    gb = jnp.concatenate([b0, b1], axis=1)

    def put(t, value):
        for b in range(4):
            out[0, :, 4 * t + b, :] = value[:, 128 * b : 128 * b + 128]

    def trailing(t):
        j = q + PCOL * t
        U = jnp.concatenate([u[c, 0, t] for c in range(KIDS)], axis=1)
        V = jnp.concatenate([kept(v[c, 0, t], rank[c, r, t]) for c in range(KIDS)], axis=1)
        acc = nt(U, V) - nt(gb, gcol[t])
        put(t, jnp.where(i >= j, acc, 0.0))

        @pl.when(i == j)
        def _():
            for e in range(PROW):
                packed[KSLAB * e : KSLAB * e + KSLAB, :] = ksum[e, t]
            for e in range(PCOL):
                at = slice(RSLAB * e, RSLAB * e + RSLAB)
                packed[at, :] = packed[at, :] + rsum[e, t]
            unpack(D, packed, True)
            add_shift(D, shift[pl.ds(j, 1), :])
            put(t, acc + D[...])

    def panel(k, C, G):
        a = lax.broadcasted_iota(jnp.int32, (N, N), 0)
        b = lax.broadcasted_iota(jnp.int32, (N, N), 1)
        pivots = jnp.sum(jnp.where(a == b, C[...], 0.0), axis=0, keepdims=True)

        @pl.when(i == k)
        def _():
            put(0, C[...] * pivots)

        @pl.when(i != k)
        def _():
            put(0, G * pivots)

    @pl.when(q > 1)
    def _():
        trailing(0)

    @pl.when(q == 0)
    def _():
        panel(0, C0, G0)

    @pl.when(q == 1)
    def _():
        panel(1, C1, G1)

    trailing(1)


def total(values):
    return functools.reduce(lambda a, b: a + b, values)


def pick(flag, value):
    return jnp.where(flag, value, jnp.zeros_like(value))


def on_device(child_u, child_v, child_rank, diag_shift):
    p = lax.axis_index("prow")
    q = lax.axis_index("pcol")
    x, core = p // 2, p % 2
    z, y = q // 4, q % 4
    both = ("prow", "pcol")
    rank = child_rank[:, :, 0, :, 0]
    u = child_u[:, :, 0, :, 0]
    v = child_v[:, :, 0, :, 0]
    meta = jnp.stack([p, q, x, core]).astype(jnp.int32)

    first, second = pl.pallas_call(
        column_kernel,
        out_shape=[shape((PACK, 128), F32)] * 2,
        in_specs=[SMEM, VMEM],
        out_specs=[VMEM] * 2,
        scratch_shapes=[pltpu.VMEM((N, KIDS * ROWS * RK), BF16)],
        compiler_params=params(32),
        cost_estimate=cost(3),
        name="column_sums",
    )(rank, v)
    parts = pl.pallas_call(
        pieces_kernel,
        out_shape=[shape((4, 4 * ROWS, 32, RK), BF16)] * 4
        + [shape((8, 4, 64, RK), BF16)]
        + [shape((8, 8, 64, RK), BF16)] * 2,
        in_specs=[SMEM, SMEM, VMEM, VMEM],
        out_specs=[VMEM] * 7,
        scratch_shapes=[pltpu.VMEM((4 * ROWS, N, RK), BF16)],
        compiler_params=params(48),
        cost_estimate=cost(4),
        name="pieces",
    )(rank, meta, u, v)
    raw, tile, cols = parts[:4], parts[4], parts[5:7]

    zgot = [lax.ppermute(raw[s], "pcol", [(k, 4 * s + k) for k in range(2)]) for s in range(1, 4)]

    tslab = lax.all_to_all(tile, "prow", 0, 0)
    first, tslab = lax.optimization_barrier((first, tslab))
    tslab = pick(q == 0, tslab[1])
    k0slab = jnp.sum(
        lax.all_to_all(first.reshape(PROW, KSLAB, 128), "prow", 0, 0), axis=0
    )
    second, _ = lax.optimization_barrier((second, k0slab))
    k1slab = jnp.sum(
        lax.all_to_all(second.reshape(PROW, KSLAB, 128), "prow", 0, 0), axis=0
    )
    got = [lax.ppermute(k0slab, "pcol", [(0, s), (1, (1 + s) % 4)]) for s in range(1, 4)]
    tgot = [lax.ppermute(tslab, "pcol", [(0, s)]) for s in range(1, 4)]
    pay = [
        pick(y == k, k0slab) + total(pick((y + 4 - k) % 4 == s, got[s - 1]) for s in range(1, 4))
        for k in range(2)
    ]
    pay, tgot = lax.optimization_barrier((pay, tgot))
    pay = pick(z == 0, jnp.concatenate(pay, axis=0))
    tpay = pick(z == 0, tslab + total(tgot))
    down = [[(i, 4 * s + i) for i in range(4)] for s in range(1, 4)]
    pay = pay + total(lax.ppermute(pay, "pcol", pairs) for pairs in down)
    tgot = [lax.ppermute(tpay, "pcol", pairs) for pairs in down]
    pay, zgot, tgot, k1slab = lax.optimization_barrier((pay, zgot, tgot, k1slab))
    tpay = tpay + total(tgot)
    turn = [
        [(2 * a + c, 2 * ((a + s) % 4) + c) for a in range(4) for c in range(2)]
        for s in range(1, 4)
    ]
    swap = [(i, i ^ 1) for i in range(8)]
    own = jnp.stack([pay] + [lax.ppermute(pay, "prow", pairs) for pairs in turn])
    town = jnp.stack([tpay] + [lax.ppermute(tpay, "prow", pairs) for pairs in turn])
    other = lax.ppermute(own, "prow", swap)
    tother = lax.ppermute(town, "prow", swap)

    hold = [
        pick(z == 0, raw[0][s]) + total(zgot[e][s] for e in range(3)) for s in range(4)
    ]
    got = [
        lax.ppermute(
            hold[s], "pcol", [(4 * a + k, 4 * a + (k + s) % 4) for a in range(4) for k in range(2)]
        )
        for s in range(1, 4)
    ]
    piece = jnp.stack(
        [
            pick(y == k, hold[0]) + total(pick((y + 4 - k) % 4 == s, got[s - 1]) for s in range(1, 4))
            for k in range(2)
        ]
    )
    rows_all = lax.all_gather(piece, "pcol")

    cols, _ = lax.optimization_barrier((cols, pay))
    arrived = [
        lax.ppermute(
            cols[h],
            both,
            [(a * PCOL + k, a * PCOL + a + 8 * (h ^ k)) for a in range(8) for k in range(2)],
        )
        for h in range(2)
    ]
    rsum = pl.pallas_call(
        row_kernel,
        out_shape=shape((PCOL, 4, RSLAB, 128), F32),
        in_specs=[SMEM, VMEM, pl.BlockSpec(memory_space=pl.ANY)],
        out_specs=VMEM,
        scratch_shapes=[pltpu.VMEM((N, 4 * RK), BF16)],
        compiler_params=params(32),
        cost_estimate=cost(4),
        name="row_sums",
    )(rank, u, k0slab)
    rsum, _ = lax.optimization_barrier((rsum, pay))
    rparts = lax.all_to_all(rsum, "pcol", 0, 0)

    own, other, town, _ = lax.optimization_barrier((own, other, town, piece))
    square = shape((N, N), F32)
    narrow = shape((N, N), BF16)
    work = pltpu.VMEM((N, N), F32)
    A0, C0, M0, K1 = pl.pallas_call(
        gather_kernel,
        out_shape=[square] * 3 + [shape((PACK, 128), F32)],
        in_specs=[SMEM] + [VMEM] * 3,
        out_specs=[VMEM] * 4,
        scratch_shapes=[pltpu.VMEM((PACK, 128), F32)],
        compiler_params=params(32),
        cost_estimate=cost(14),
        name="first_pivot_a",
    )(meta, own, other, diag_shift)
    arrived, rparts, _ = lax.optimization_barrier((arrived, rparts, A0))
    rown = jnp.sum(rparts, axis=0)
    rown = jnp.concatenate(
        [
            jnp.broadcast_to(jnp.stack([rown[h], rown[2 + h]]), (8, COLS, RSLAB, 128))
            for h in range(2)
        ],
        axis=0,
    )
    side = q // 8
    hold = [jnp.where(side == 0, arrived[k], arrived[1 - k]) for k in range(2)]
    share = lax.all_to_all(jnp.stack(hold, axis=1), "prow", 0, 0)
    A0, hold, rown = lax.optimization_barrier((A0, hold, rown))
    C0, M0h, M0l, g01, A1 = pl.pallas_call(
        first_kernel,
        out_shape=[square, narrow, narrow, narrow, square],
        in_specs=[SMEM] + [VMEM] * 7,
        out_specs=[VMEM] * 5,
        scratch_shapes=[work, work, pltpu.VMEM((4, N, RK), BF16)],
        compiler_params=params(32),
        cost_estimate=cost(15),
        name="first_pivot_b",
    )(meta, A0, C0, M0, K1, town, tother, diag_shift)
    share, _ = lax.optimization_barrier((share, A1))
    share = lax.dynamic_index_in_dim(share, q % PROW, 0, keepdims=False)
    A1, share = lax.optimization_barrier((A1, share))
    cols_all = lax.all_gather(share, "prow")
    kslab, _ = lax.optimization_barrier((jnp.stack([k0slab, k1slab]), A1))
    kall = lax.all_to_all(jnp.broadcast_to(kslab, (PROW, COLS, KSLAB, 128)), "prow", 0, 0)
    A1, C1, M1 = pl.pallas_call(
        half_kernel,
        out_shape=[square] * 3,
        in_specs=[VMEM],
        out_specs=[VMEM] * 3,
        compiler_params=params(32),
        cost_estimate=cost(13),
        name="second_pivot_a",
    )(A1)
    rown, _ = lax.optimization_barrier((rown, A1))
    rall = lax.all_to_all(rown, "pcol", 0, 0)
    A1, kall, rows_all = lax.optimization_barrier((A1, kall, rows_all))
    C1, M1h, M1l, X1h, X1l = pl.pallas_call(
        second_kernel,
        out_shape=[square] + [narrow] * 4,
        in_specs=[VMEM] * 4,
        out_specs=[VMEM] * 5,
        scratch_shapes=[work, work],
        compiler_params=params(32),
        cost_estimate=cost(13),
        name="second_pivot_b",
    )(A1, C1, M1, g01)
    tiles = pl.BlockSpec((KIDS, 1, COLS, N, RK), lambda r: (0, r, 0, 0, 0))
    out = pl.pallas_call(
        final_kernel,
        grid=(ROWS,),
        out_shape=shape((ROWS, N, COLS * 4, 128), F32),
        in_specs=[SMEM, SMEM, VMEM, tiles, tiles] + [VMEM] * 12,
        out_specs=pl.BlockSpec((1, N, COLS * 4, 128), lambda r: (r, 0, 0, 0)),
        scratch_shapes=[
            pltpu.VMEM((COLS, N, 2 * N), BF16),
            pltpu.VMEM((PACK, 128), F32),
            pltpu.VMEM((N, N), F32),
        ],
        compiler_params=params(60),
        cost_estimate=cost(35),
        name="panels_and_update",
    )(rank, meta, diag_shift, u, v, rows_all, cols_all, rall, kall,
      C0, M0h, M0l, C1, M1h, M1l, X1h, X1l)
    return out.reshape(ROWS, 1, N, COLS, 1, N)


def solution(mesh):
    placed = (
        P(None, None, "prow", None, "pcol", None, None),
        P(None, None, "prow", None, "pcol", None, None),
        P(None, None, "prow", None, "pcol"),
        P(),
    )
    return jax.shard_map(
        on_device,
        mesh=mesh,
        in_specs=placed,
        out_specs=P(None, "prow", None, None, "pcol", None),
        check_vma=False,
    )
```

```python
import functools
import jax
import jax.numpy as jnp
from jax import lax
from jax.experimental import pallas as pl
from jax.experimental.pallas import tpu as pltpu
from jax.sharding import PartitionSpec as P

F32 = jnp.float32
BF16 = jnp.bfloat16
PROW, PCOL = 8, 16
ROWS, COLS, KIDS = 5, 2, 2
N, RK = 512, 128
TRI = [(a, b) for a in range(4) for b in range(a + 1)]
PACK = 128 * len(TRI)
KSLAB = PACK // PROW
RSLAB = PACK // PCOL
VMEM = pl.BlockSpec(memory_space=pltpu.VMEM)
SMEM = pl.BlockSpec(memory_space=pltpu.SMEM)
EXACT = lax.Precision.HIGHEST


def shape(dims, dtype):
    return jax.ShapeDtypeStruct(dims, dtype)


def cost(us):
    return pl.CostEstimate(flops=us * 1_000_000_000, transcendentals=0, bytes_accessed=1 << 20)


def params(mib):
    return pltpu.CompilerParams(vmem_limit_bytes=mib << 20)


def nt(a, b, precision=None):
    return lax.dot_general(
        a, b, (((1,), (1,)), ((), ())), precision=precision, preferred_element_type=F32
    )


def nn(a, b, precision=None):
    return lax.dot_general(
        a, b, (((1,), (0,)), ((), ())), precision=precision, preferred_element_type=F32
    )


def halves(x):
    hi = x.astype(BF16)
    return hi, (x - hi.astype(F32)).astype(BF16)


def kept(tile, rank):
    lane = lax.broadcasted_iota(jnp.int32, tile.shape, 1)
    return jnp.where(lane < rank, tile, jnp.zeros_like(tile))


def column_kernel(rank, v, first, second, cat):
    for t, out in enumerate((first, second)):
        for c in range(KIDS):
            for r in range(ROWS):
                at = (c * ROWS + r) * RK
                cat[:, at : at + RK] = kept(v[c, r, t], rank[c, r, t])
        total = nt(cat[...], cat[...])
        for n, (a, b) in enumerate(TRI):
            out[128 * n : 128 * n + 128, :] = total[
                128 * a : 128 * a + 128, 128 * b : 128 * b + 128
            ]


def pieces_kernel(rank, meta, u, v, _, *refs):
    raw, tile, cols, masked = refs[:4], refs[4:6], refs[6:8], refs[8]
    root = jnp.where(meta[1] == 1, 1, 0)
    for c in range(KIDS):
        for r in range(ROWS):
            masked[c * ROWS + r] = kept(u[c, r, 0], rank[c, r, 0])
            masked[(KIDS + c) * ROWS + r] = kept(v[c, r, 0], rank[c, r, 0])
    for s in range(16):
        raw[s // 4][s % 4] = masked[:, 32 * s : 32 * s + 32, :]
    for s in range(8):
        part = slice(64 * s, 64 * s + 64)
        for a in range(2 * KIDS):
            tile[s // 4][a, 64 * (s % 4) : 64 * (s % 4) + 64, :] = masked[a * ROWS, part, :]
            for h in range(2):
                row = lax.rem(root + h, 2)
                cols[h][s, a] = masked[a * ROWS + row, part, :]
                cols[h][s, 4 + a] = masked[a * ROWS + 2 + row, part, :]


def row_kernel(rank, u, _, rsum, cat):
    for r in range(4):
        for c in range(KIDS):
            for t in range(COLS):
                at = (2 * c + t) * RK
                cat[:, at : at + RK] = kept(u[c, r, t], rank[c, r, t])
        total = nt(cat[...], cat[...])
        for n, (a, b) in enumerate(TRI):
            for e in range(128 // 16):
                line = 128 * n + 16 * e
                rsum[line // RSLAB, r, line % RSLAB : line % RSLAB + 16, :] = total[
                    128 * a + 16 * e : 128 * a + 16 * e + 16, 128 * b : 128 * b + 128
                ]


def base_inverse(block):
    lane = lax.broadcasted_iota(jnp.int32, (8, 128), 1)
    sub = lax.broadcasted_iota(jnp.int32, (8, 128), 0)
    rows = [block[8 * v : 8 * v + 8, :] for v in range(16)]

    def wide(x):
        return jnp.broadcast_to(x, (8, 128))

    for J in range(16):
        inside = (lane >= 8 * J) & (lane < 8 * J + 8)
        B = [wide(rows[J][:, 8 * J + n : 8 * J + n + 1]) for n in range(8)]
        fwd = jnp.where(inside, jnp.where(lane - 8 * J == sub, 1.0, 0.0), rows[J])
        full = fwd
        roots = jnp.zeros((8, 128), F32)
        for k in range(8):
            r = lax.rsqrt(wide(B[k][k : k + 1, :]))
            row = wide(full[k : k + 1, :])
            mult = jnp.where(sub == k, 0.0, B[k] * (r * r))
            full = full - mult * row
            fwd = fwd - jnp.where(sub > k, mult, 0.0) * row
            for n in range(k + 1, 8):
                B[n] = B[n] - mult * wide(B[n][k : k + 1, :])
            roots = jnp.where(sub == k, r, roots)
        rows[J] = fwd * roots
        scaled = full * (roots * roots)
        Y = [wide(scaled[n : n + 1, :]) for n in range(8)]
        for v in range(J + 1, 16):
            b = [wide(rows[v][:, 8 * J + n : 8 * J + n + 1]) * Y[n] for n in range(8)]
            t = ((b[0] + b[1]) + (b[2] + b[3])) + ((b[4] + b[5]) + (b[6] + b[7]))
            rows[v] = jnp.where(inside, 0.0, rows[v]) - t
    return jnp.concatenate(
        [jnp.where(lane <= sub + 8 * v, rows[v], 0.0) for v in range(16)], axis=0
    )


def factor(A, C, M, steps):
    i = lax.broadcasted_iota(jnp.int32, (128, 128), 0)
    j = lax.broadcasted_iota(jnp.int32, (128, 128), 1)
    if steps[0] == 0:
        M[...] = jnp.zeros_like(M)
        C[...] = jnp.zeros_like(C)
    for b in steps:
        at = slice(128 * b, 128 * b + 128)
        inv = base_inverse(A[at, at])
        if b:
            left = nn(C[at, 0 : 128 * b], M[0 : 128 * b, 0 : 128 * b], EXACT)
            M[at, 0 : 128 * b] = -nn(inv, left, EXACT)
        M[at, at] = inv
        C[at, at] = jnp.where(i >= j, nt(A[at, at], inv, EXACT), 0.0)
        if b < 3:
            below = slice(128 * b + 128, N)
            panel = nt(A[below, at], inv, EXACT)
            C[below, at] = panel
            A[below, below] = A[below, below] - nt(panel, panel, EXACT)


def add_shift(A, line):
    i = lax.broadcasted_iota(jnp.int32, (N, N), 0)
    j = lax.broadcasted_iota(jnp.int32, (N, N), 1)
    A[...] = A[...] + jnp.where(i == j, line, 0.0)


def unpack(A, packed, mirror):
    for n, (a, b) in enumerate(TRI):
        block = packed[128 * n : 128 * n + 128, :]
        A[128 * a : 128 * a + 128, 128 * b : 128 * b + 128] = block
        if a != b:
            A[128 * b : 128 * b + 128, 128 * a : 128 * a + 128] = (
                block.T if mirror else jnp.zeros_like(block)
            )


def gather_kernel(meta, own, other, shift, A, C, M, K1, packed):
    x, core = meta[2], meta[3]
    for s in range(4):
        chip = lax.rem(x - s + 4, 4)
        for part, lane in ((own, core), (other, 1 - core)):
            place = 2 * chip + lane
            at = pl.ds(pl.multiple_of(place * KSLAB, 8), KSLAB)
            packed[at, :] = part[s, 0:KSLAB, :]
            K1[at, :] = part[s, KSLAB : 2 * KSLAB, :]
    unpack(A, packed, False)
    add_shift(A, shift[0:1, :])
    factor(A, C, M, (0, 1))


def take(refs, into):
    for ref, scratch in zip(refs, into):
        scratch[...] = ref[...]


def first_kernel(
    meta, A0, C0, M0, K1, town, tother, shift, C, Mh, Ml, Gb, A1, A, M, tile
):
    core = meta[3]
    for part, lane in ((town, core), (tother, 1 - core)):
        line = pl.multiple_of(lane * 256, 16)
        for a in range(4):
            tile[a, pl.ds(line, 256), :] = part[a]
    take((A0, C0, M0), (A, C, M))
    factor(A, C, M, (2, 3))
    hi, lo = halves(M[...])
    Mh[...] = hi
    Ml[...] = lo
    U = jnp.concatenate([tile[0], tile[1]], axis=1)
    V = jnp.concatenate([tile[2], tile[3]], axis=1)
    wh, wl = halves(nn(hi, V) + nn(lo, V))
    G = (nt(U, wh) + nt(U, wl)).astype(BF16)
    Gb[...] = G
    unpack(A, K1, False)
    add_shift(A, shift[1:2, :])
    A1[...] = A[...] + (nt(U, U) - nt(G, G))


def half_kernel(A1, A, C, M):
    A[...] = A1[...]
    factor(A, C, M, (0, 1))


def second_kernel(A1, C1, M1, Gb, C, Mh, Ml, Xh, Xl, A, M):
    take((A1, C1, M1), (A, C, M))
    factor(A, C, M, (2, 3))
    hi, lo = halves(M[...])
    Mh[...] = hi
    Ml[...] = lo
    xh, xl = halves(nn(hi, Gb[...]) + nn(lo, Gb[...]))
    Xh[...] = xh
    Xl[...] = xl


def solve(i, tiles, M0h, M0l, M1h, M1l, X1h, X1l):
    U0, V0, U1, V1 = tiles
    wh, wl = halves(nn(M0h[...], V0) + nn(M0l[...], V0))
    G0 = jnp.where(i > 0, nt(U0, wh) + nt(U0, wl), 0.0)
    b0 = G0.astype(BF16)
    wh, wl = halves(nn(M1h[...], V1) + nn(M1l[...], V1))
    G1 = (nt(U1, wh) + nt(U1, wl)) - (nt(b0, X1h[...]) + nt(b0, X1l[...]))
    G1 = jnp.where(i > 1, G1, 0.0)
    return G0, G1, b0, G1.astype(BF16)


def pair(get, first):
    return jnp.concatenate([get(first), get(first + 1)], axis=1)


def panel_kernel(meta, rb, C0, M0h, M0l, C1, M1h, M1l, X1h, X1l, gb, side):
    r = pl.program_id(0)
    p, q = meta[0], meta[1]
    i = r * PROW + p
    tiles = []
    for k in range(2):
        def get(a, k=k):
            whole = rb[:, k, a * ROWS + r]
            if k:
                order = [4 * zz + yy for zz in range(4) for yy in (1, 2, 3, 0)]
                whole = jnp.concatenate([whole[e : e + 1] for e in order], axis=0)
            return whole.reshape(N, RK)
        tiles += [pair(get, 0), pair(get, 2)]
    G0, G1, b0, b1 = solve(i, tiles, M0h, M0l, M1h, M1l, X1h, X1l)
    gb[0, :, 0:N] = b0
    gb[0, :, N : 2 * N] = b1

    def panel(k, C, G):
        a = lax.broadcasted_iota(jnp.int32, (N, N), 0)
        b = lax.broadcasted_iota(jnp.int32, (N, N), 1)
        pivots = jnp.sum(jnp.where(a == b, C[...], 0.0), axis=0, keepdims=True)

        @pl.when(i == k)
        def _():
            side[0] = C[...] * pivots

        @pl.when(i != k)
        def _():
            side[0] = G * pivots

    @pl.when(q == 0)
    def _():
        panel(0, C0, G0)

    @pl.when(q == 1)
    def _():
        panel(1, C1, G1)

    @pl.when(q > 1)
    def _():
        side[...] = jnp.zeros_like(side)


def final_kernel(
    rank, meta, shift, u, v, gb, side, rc, rsum, ksum,
    M0h, M0l, M1h, M1l, X1h, X1l, out, gcol, packed, D
):
    r = pl.program_id(0)
    p, q = meta[0], meta[1]

    @pl.when(r == 0)
    def _():
        for t in range(COLS):
            tiles = []
            for k in range(2):
                def get(a, k=k, t=t):
                    return jnp.concatenate(
                        [rc[s, k, 4 * t + a] for s in range(PROW)], axis=0
                    )
                tiles += [pair(get, 0), pair(get, 2)]
            _, _, b0, b1 = solve(q + PCOL * t, tiles, M0h, M0l, M1h, M1l, X1h, X1l)
            gcol[t, :, 0:N] = b0
            gcol[t, :, N : 2 * N] = b1

    i = r * PROW + p

    def put(t, value):
        for b in range(4):
            out[0, :, 4 * t + b, :] = value[:, 128 * b : 128 * b + 128]

    def trailing(t):
        j = q + PCOL * t
        U = jnp.concatenate([u[c, 0, t] for c in range(KIDS)], axis=1)
        V = jnp.concatenate([kept(v[c, 0, t], rank[c, r, t]) for c in range(KIDS)], axis=1)
        acc = nt(U, V) - nt(gb[0], gcol[t])
        put(t, jnp.where(i >= j, acc, 0.0))

        @pl.when(i == j)
        def _():
            for e in range(PROW):
                packed[KSLAB * e : KSLAB * e + KSLAB, :] = ksum[e, t]
            for e in range(PCOL):
                at = slice(RSLAB * e, RSLAB * e + RSLAB)
                packed[at, :] = packed[at, :] + rsum[e, t]
            unpack(D, packed, True)
            add_shift(D, shift[pl.ds(j, 1), :])
            put(t, acc + D[...])

    @pl.when(q > 1)
    def _():
        trailing(0)

    @pl.when(q <= 1)
    def _():
        put(0, side[0])

    trailing(1)


def total(values):
    return functools.reduce(lambda a, b: a + b, values)


def pick(flag, value):
    return jnp.where(flag, value, jnp.zeros_like(value))


def on_device(child_u, child_v, child_rank, diag_shift):
    p = lax.axis_index("prow")
    q = lax.axis_index("pcol")
    x, core = p // 2, p % 2
    z, y = q // 4, q % 4
    both = ("prow", "pcol")
    rank = child_rank[:, :, 0, :, 0]
    u = child_u[:, :, 0, :, 0]
    v = child_v[:, :, 0, :, 0]
    meta = jnp.stack([p, q, x, core]).astype(jnp.int32)

    first, second = pl.pallas_call(
        column_kernel,
        out_shape=[shape((PACK, 128), F32)] * 2,
        in_specs=[SMEM, VMEM],
        out_specs=[VMEM] * 2,
        scratch_shapes=[pltpu.VMEM((N, KIDS * ROWS * RK), BF16)],
        compiler_params=params(32),
        cost_estimate=cost(3),
        name="column_sums",
    )(rank, v)
    parts = pl.pallas_call(
        pieces_kernel,
        out_shape=[shape((4, 4 * ROWS, 32, RK), BF16)] * 4
        + [shape((4, 256, RK), BF16)] * 2
        + [shape((8, 8, 64, RK), BF16)] * 2,
        in_specs=[SMEM, SMEM, VMEM, VMEM, pl.BlockSpec(memory_space=pl.ANY)],
        out_specs=[VMEM] * 8,
        scratch_shapes=[pltpu.VMEM((4 * ROWS, N, RK), BF16)],
        compiler_params=params(48),
        cost_estimate=cost(4),
        name="pieces",
    )(rank, meta, u, v, second)
    raw, tile, cols = parts[:4], parts[4:6], parts[6:8]
    swap = [(i, i ^ 1) for i in range(8)]
    turn = [
        [(2 * a + c, 2 * ((a + s) % 4) + c) for a in range(4) for c in range(2)]
        for s in range(1, 4)
    ]
    down = [[(i, 4 * s + i) for i in range(4)] for s in range(1, 4)]

    kgot = lax.all_to_all(first.reshape(PROW, KSLAB, 128), "prow", 0, 0)
    tgot = [
        [lax.ppermute(half, both, [(PCOL, PCOL + s)]) for s in range(1, 4)] for half in tile
    ]
    zgot = [lax.ppermute(raw[s], "pcol", [(k, 4 * s + k) for k in range(2)]) for s in range(1, 4)]
    arrived = [
        lax.ppermute(
            cols[h],
            both,
            [(a * PCOL + k, a * PCOL + a + 8 * (h ^ k)) for a in range(8) for k in range(2)],
        )
        for h in range(2)
    ]
    k0slab = jnp.sum(kgot, axis=0)

    got = [lax.ppermute(k0slab, "pcol", [(0, s), (1, (1 + s) % 4)]) for s in range(1, 4)]
    got, tgot, zgot = lax.optimization_barrier((got, tgot, zgot))
    pay = [
        pick(y == k, k0slab) + total(pick((y + 4 - k) % 4 == s, got[s - 1]) for s in range(1, 4))
        for k in range(2)
    ]
    pay = pick(z == 0, jnp.concatenate(pay, axis=0))
    tpay = jnp.stack([pick((p == 1) & (q == 0), tile[h]) + total(tgot[h]) for h in range(2)])
    tgot = [
        lax.ppermute(tpay, both, [(PCOL + i, PCOL + 4 * s + i) for i in range(4)])
        for s in range(1, 4)
    ]

    got = [lax.ppermute(pay, "pcol", pairs) for pairs in down]
    hold = [
        pick(z == 0, raw[0][s]) + total(zgot[e][s] for e in range(3)) for s in range(4)
    ]
    ygot = [
        lax.ppermute(
            hold[s], "pcol", [(4 * a + k, 4 * a + (k + s) % 4) for a in range(4) for k in range(2)]
        )
        for s in range(1, 4)
    ]
    got, arrived, tgot, ygot = lax.optimization_barrier((got, arrived, tgot, ygot))
    pay = pay + total(got)
    piece = jnp.stack(
        [
            pick(y == k, hold[0]) + total(pick((y + 4 - k) % 4 == s, ygot[s - 1]) for s in range(1, 4))
            for k in range(2)
        ]
    )
    rows_all = lax.all_gather(piece, "pcol")
    tpay = pick(z == 0, tpay) + total(tgot)
    thalf = jnp.where(core == 1, tpay[1], lax.ppermute(tpay[0], "prow", [(1, 0)]))

    got = [lax.ppermute(pay, "prow", pairs) for pairs in turn]
    tgot = [
        lax.ppermute(thalf, "prow", [(c, 2 * s + c) for c in range(2)]) for s in range(1, 4)
    ]
    side = q // 8
    hold = jnp.stack(
        [jnp.where(side == 0, arrived[k], arrived[1 - k]) for k in range(2)], axis=1
    )
    rsum = pl.pallas_call(
        row_kernel,
        out_shape=shape((PCOL, 4, RSLAB, 128), F32),
        in_specs=[SMEM, VMEM, pl.BlockSpec(memory_space=pl.ANY)],
        out_specs=VMEM,
        scratch_shapes=[pltpu.VMEM((N, 4 * RK), BF16)],
        compiler_params=params(32),
        cost_estimate=cost(4),
        name="row_sums",
    )(rank, u, k0slab)
    got, piece, hold, rsum = lax.optimization_barrier((got, piece, hold, rsum))
    share = lax.all_to_all(hold, "prow", 0, 0)
    own = jnp.stack([pay] + got)
    other = lax.ppermute(own, "prow", swap)
    own, other, tgot = lax.optimization_barrier((own, other, tgot))
    thalf = pick(x == 0, thalf) + total(tgot)
    tother = lax.ppermute(thalf, "prow", swap)
    own, thalf = lax.optimization_barrier((own, thalf))

    square = shape((N, N), F32)
    narrow = shape((N, N), BF16)
    work = pltpu.VMEM((N, N), F32)
    A0, C0, M0, K1 = pl.pallas_call(
        gather_kernel,
        out_shape=[square] * 3 + [shape((PACK, 128), F32)],
        in_specs=[SMEM] + [VMEM] * 3,
        out_specs=[VMEM] * 4,
        scratch_shapes=[pltpu.VMEM((PACK, 128), F32)],
        compiler_params=params(32),
        cost_estimate=cost(14),
        name="first_pivot_a",
    )(meta, own, other, diag_shift)
    share, _ = lax.optimization_barrier((share, A0))
    share = lax.dynamic_index_in_dim(share, q % PROW, 0, keepdims=False)
    cols_all = lax.all_gather(share, "prow")
    rsum, share = lax.optimization_barrier((rsum, share))
    rparts = lax.all_to_all(rsum, "pcol", 0, 0)
    A0, share = lax.optimization_barrier((A0, share))
    C0, M0h, M0l, g01, A1 = pl.pallas_call(
        first_kernel,
        out_shape=[square, narrow, narrow, narrow, square],
        in_specs=[SMEM] + [VMEM] * 7,
        out_specs=[VMEM] * 5,
        scratch_shapes=[work, work, pltpu.VMEM((4, N, RK), BF16)],
        compiler_params=params(32),
        cost_estimate=cost(15),
        name="first_pivot_b",
    )(meta, A0, C0, M0, K1, thalf, tother, diag_shift)
    A1, C1, M1 = pl.pallas_call(
        half_kernel,
        out_shape=[square] * 3,
        in_specs=[VMEM],
        out_specs=[VMEM] * 3,
        compiler_params=params(32),
        cost_estimate=cost(13),
        name="second_pivot_a",
    )(A1)
    rparts, second, A1 = lax.optimization_barrier((rparts, second, A1))
    kgot = lax.all_to_all(second.reshape(PROW, KSLAB, 128), "prow", 0, 0)
    rown = jnp.sum(rparts, axis=0)
    rown = jnp.concatenate(
        [
            jnp.broadcast_to(jnp.stack([rown[h], rown[2 + h]]), (8, COLS, RSLAB, 128))
            for h in range(2)
        ],
        axis=0,
    )
    A1, rown = lax.optimization_barrier((A1, rown))
    C1, M1h, M1l, X1h, X1l = pl.pallas_call(
        second_kernel,
        out_shape=[square] + [narrow] * 4,
        in_specs=[VMEM] * 4,
        out_specs=[VMEM] * 5,
        scratch_shapes=[work, work],
        compiler_params=params(32),
        cost_estimate=cost(13),
        name="second_pivot_b",
    )(A1, C1, M1, g01)
    kgot, rown, rows_all, C1 = lax.optimization_barrier((kgot, rown, rows_all, C1))
    kall = lax.all_gather(jnp.stack([k0slab, jnp.sum(kgot, axis=0)]), "prow")
    rall = lax.all_to_all(rown, "pcol", 0, 0)
    gb, panels = pl.pallas_call(
        panel_kernel,
        grid=(ROWS,),
        out_shape=[shape((ROWS, N, 2 * N), BF16), shape((ROWS, N, N), F32)],
        in_specs=[SMEM] + [VMEM] * 9,
        out_specs=[
            pl.BlockSpec((1, N, 2 * N), lambda r: (r, 0, 0)),
            pl.BlockSpec((1, N, N), lambda r: (r, 0, 0)),
        ],
        compiler_params=params(48),
        cost_estimate=cost(17),
        name="panels",
    )(meta, rows_all, C0, M0h, M0l, C1, M1h, M1l, X1h, X1l)
    tiles = pl.BlockSpec((KIDS, 1, COLS, N, RK), lambda r: (0, r, 0, 0, 0))
    out = pl.pallas_call(
        final_kernel,
        grid=(ROWS,),
        out_shape=shape((ROWS, N, COLS * 4, 128), F32),
        in_specs=[
            SMEM,
            SMEM,
            VMEM,
            tiles,
            tiles,
            pl.BlockSpec((1, N, 2 * N), lambda r: (r, 0, 0)),
            pl.BlockSpec((1, N, N), lambda r: (r, 0, 0)),
        ]
        + [VMEM] * 9,
        out_specs=pl.BlockSpec((1, N, COLS * 4, 128), lambda r: (r, 0, 0, 0)),
        scratch_shapes=[
            pltpu.VMEM((COLS, N, 2 * N), BF16),
            pltpu.VMEM((PACK, 128), F32),
            pltpu.VMEM((N, N), F32),
        ],
        compiler_params=params(60),
        cost_estimate=cost(20),
        name="update",
    )(rank, meta, diag_shift, u, v, gb, panels, cols_all, rall, kall,
      M0h, M0l, M1h, M1l, X1h, X1l)
    return out.reshape(ROWS, 1, N, COLS, 1, N)


def solution(mesh):
    placed = (
        P(None, None, "prow", None, "pcol", None, None),
        P(None, None, "prow", None, "pcol", None, None),
        P(None, None, "prow", None, "pcol"),
        P(),
    )
    return jax.shard_map(
        on_device,
        mesh=mesh,
        in_specs=placed,
        out_specs=P(None, "prow", None, None, "pcol", None),
        check_vma=False,
    )
```

```python
import functools
import jax
import jax.numpy as jnp
from jax import lax
from jax.experimental import pallas as pl
from jax.experimental.pallas import tpu as pltpu
from jax.sharding import PartitionSpec as P

F32 = jnp.float32
BF16 = jnp.bfloat16
PROW, PCOL = 8, 16
ROWS, COLS, KIDS = 5, 2, 2
N, RK = 512, 128
TRI = [(a, b) for a in range(4) for b in range(a + 1)]
PACK = 128 * len(TRI)
KSLAB = PACK // PROW
RSLAB = PACK // PCOL
VMEM = pl.BlockSpec(memory_space=pltpu.VMEM)
SMEM = pl.BlockSpec(memory_space=pltpu.SMEM)
EXACT = lax.Precision.HIGHEST


def shape(dims, dtype):
    return jax.ShapeDtypeStruct(dims, dtype)


def cost(us):
    return pl.CostEstimate(flops=us * 1_000_000_000, transcendentals=0, bytes_accessed=1 << 20)


def params(mib):
    return pltpu.CompilerParams(vmem_limit_bytes=mib << 20)


def nt(a, b, precision=None):
    return lax.dot_general(
        a, b, (((1,), (1,)), ((), ())), precision=precision, preferred_element_type=F32
    )


def nn(a, b, precision=None):
    return lax.dot_general(
        a, b, (((1,), (0,)), ((), ())), precision=precision, preferred_element_type=F32
    )


def halves(x):
    hi = x.astype(BF16)
    return hi, (x - hi.astype(F32)).astype(BF16)


def kept(tile, rank):
    lane = lax.broadcasted_iota(jnp.int32, tile.shape, 1)
    return jnp.where(lane < rank, tile, jnp.zeros_like(tile))


def column_kernel(rank, v, out, cat, packed):
    for t in range(COLS):
        for c in range(KIDS):
            for r in range(ROWS):
                at = (c * ROWS + r) * RK
                cat[:, at : at + RK] = kept(v[c, r, t], rank[c, r, t])
        total = nt(cat[...], cat[...])
        for n, (a, b) in enumerate(TRI):
            packed[128 * n : 128 * n + 128, :] = total[
                128 * a : 128 * a + 128, 128 * b : 128 * b + 128
            ]
        for s in range(PROW):
            out[s, t] = packed[KSLAB * s : KSLAB * s + KSLAB, :]


def pieces_kernel(rank, meta, u, v, _, *refs):
    raw, tile, cols, masked = refs[:4], refs[4], refs[5:7], refs[7]
    root = jnp.where(meta[1] == 1, 1, 0)
    for c in range(KIDS):
        for r in range(ROWS):
            masked[c * ROWS + r] = kept(u[c, r, 0], rank[c, r, 0])
            masked[(KIDS + c) * ROWS + r] = kept(v[c, r, 0], rank[c, r, 0])
    for s in range(16):
        raw[s // 4][s % 4] = masked[:, 32 * s : 32 * s + 32, :]
    for s in range(8):
        part = slice(64 * s, 64 * s + 64)
        for a in range(2 * KIDS):
            tile[s // 4, a, 64 * (s % 4) : 64 * (s % 4) + 64, :] = masked[a * ROWS, part, :]
            for h in range(2):
                row = lax.rem(root + h, 2)
                cols[h][s, a] = masked[a * ROWS + row, part, :]
                cols[h][s, 4 + a] = masked[a * ROWS + 2 + row, part, :]


def row_kernel(rank, u, _, rsum, cat):
    for r in range(4):
        for c in range(KIDS):
            for t in range(COLS):
                at = (2 * c + t) * RK
                cat[:, at : at + RK] = kept(u[c, r, t], rank[c, r, t])
        total = nt(cat[...], cat[...])
        for n, (a, b) in enumerate(TRI):
            for e in range(128 // 16):
                line = 128 * n + 16 * e
                rsum[line // RSLAB, r, line % RSLAB : line % RSLAB + 16, :] = total[
                    128 * a + 16 * e : 128 * a + 16 * e + 16, 128 * b : 128 * b + 128
                ]


def base_inverse(block):
    lane = lax.broadcasted_iota(jnp.int32, (8, 128), 1)
    sub = lax.broadcasted_iota(jnp.int32, (8, 128), 0)
    rows = [block[8 * v : 8 * v + 8, :] for v in range(16)]

    def wide(x):
        return jnp.broadcast_to(x, (8, 128))

    for J in range(16):
        inside = (lane >= 8 * J) & (lane < 8 * J + 8)
        B = [wide(rows[J][:, 8 * J + n : 8 * J + n + 1]) for n in range(8)]
        fwd = jnp.where(inside, jnp.where(lane - 8 * J == sub, 1.0, 0.0), rows[J])
        full = fwd
        roots = jnp.zeros((8, 128), F32)
        for k in range(8):
            r = lax.rsqrt(wide(B[k][k : k + 1, :]))
            row = wide(full[k : k + 1, :])
            mult = jnp.where(sub == k, 0.0, B[k] * (r * r))
            full = full - mult * row
            fwd = fwd - jnp.where(sub > k, mult, 0.0) * row
            for n in range(k + 1, 8):
                B[n] = B[n] - mult * wide(B[n][k : k + 1, :])
            roots = jnp.where(sub == k, r, roots)
        rows[J] = fwd * roots
        scaled = full * (roots * roots)
        Y = [wide(scaled[n : n + 1, :]) for n in range(8)]
        for v in range(J + 1, 16):
            b = [wide(rows[v][:, 8 * J + n : 8 * J + n + 1]) * Y[n] for n in range(8)]
            t = ((b[0] + b[1]) + (b[2] + b[3])) + ((b[4] + b[5]) + (b[6] + b[7]))
            rows[v] = jnp.where(inside, 0.0, rows[v]) - t
    return jnp.concatenate(
        [jnp.where(lane <= sub + 8 * v, rows[v], 0.0) for v in range(16)], axis=0
    )


def factor(A, C, M, steps):
    i = lax.broadcasted_iota(jnp.int32, (128, 128), 0)
    j = lax.broadcasted_iota(jnp.int32, (128, 128), 1)
    if steps[0] == 0:
        M[...] = jnp.zeros_like(M)
        C[...] = jnp.zeros_like(C)
    for b in steps:
        at = slice(128 * b, 128 * b + 128)
        inv = base_inverse(A[at, at])
        if b:
            left = nn(C[at, 0 : 128 * b], M[0 : 128 * b, 0 : 128 * b], EXACT)
            M[at, 0 : 128 * b] = -nn(inv, left, EXACT)
        M[at, at] = inv
        C[at, at] = jnp.where(i >= j, nt(A[at, at], inv, EXACT), 0.0)
        if b < 3:
            below = slice(128 * b + 128, N)
            panel = nt(A[below, at], inv, EXACT)
            C[below, at] = panel
            A[below, below] = A[below, below] - nt(panel, panel, EXACT)


def add_shift(A, line):
    i = lax.broadcasted_iota(jnp.int32, (N, N), 0)
    j = lax.broadcasted_iota(jnp.int32, (N, N), 1)
    A[...] = A[...] + jnp.where(i == j, line, 0.0)


def unpack(A, packed, mirror):
    for n, (a, b) in enumerate(TRI):
        block = packed[128 * n : 128 * n + 128, :]
        A[128 * a : 128 * a + 128, 128 * b : 128 * b + 128] = block
        if a != b:
            A[128 * b : 128 * b + 128, 128 * a : 128 * a + 128] = (
                block.T if mirror else jnp.zeros_like(block)
            )


def first_kernel(
    meta, own, other, town, tother, shift, C, Mh, Ml, Gb, A1, packed, K1, A, M, tile
):
    x, core = meta[2], meta[3]
    for s in range(4):
        chip = lax.rem(x - s + 4, 4)
        for part, lane in ((own, core), (other, 1 - core)):
            place = 2 * chip + lane
            at = pl.ds(pl.multiple_of(place * KSLAB, 8), KSLAB)
            packed[at, :] = part[s, 0:KSLAB, :]
            K1[at, :] = part[s, KSLAB : 2 * KSLAB, :]
    unpack(A, packed, False)
    add_shift(A, shift[0:1, :])
    factor(A, C, M, (0, 1, 2, 3))
    for part, lane in ((town, core), (tother, 1 - core)):
        line = pl.multiple_of(lane * 256, 16)
        for a in range(4):
            tile[a, pl.ds(line, 256), :] = part[a]
    hi, lo = halves(M[...])
    Mh[...] = hi
    Ml[...] = lo
    U = jnp.concatenate([tile[0], tile[1]], axis=1)
    V = jnp.concatenate([tile[2], tile[3]], axis=1)
    wh, wl = halves(nn(hi, V) + nn(lo, V))
    G = (nt(U, wh) + nt(U, wl)).astype(BF16)
    Gb[...] = G
    unpack(A, K1, False)
    add_shift(A, shift[1:2, :])
    A1[...] = A[...] + (nt(U, U) - nt(G, G))


def second_kernel(A1, Gb, C, Mh, Ml, Xh, Xl, A, M):
    A[...] = A1[...]
    factor(A, C, M, (0, 1, 2, 3))
    hi, lo = halves(M[...])
    Mh[...] = hi
    Ml[...] = lo
    xh, xl = halves(nn(hi, Gb[...]) + nn(lo, Gb[...]))
    Xh[...] = xh
    Xl[...] = xl


def solve(i, tiles, M0h, M0l, M1h, M1l, X1h, X1l):
    U0, V0, U1, V1 = tiles
    wh, wl = halves(nn(M0h[...], V0) + nn(M0l[...], V0))
    G0 = jnp.where(i > 0, nt(U0, wh) + nt(U0, wl), 0.0)
    b0 = G0.astype(BF16)
    wh, wl = halves(nn(M1h[...], V1) + nn(M1l[...], V1))
    G1 = (nt(U1, wh) + nt(U1, wl)) - (nt(b0, X1h[...]) + nt(b0, X1l[...]))
    G1 = jnp.where(i > 1, G1, 0.0)
    return G0, G1, b0, G1.astype(BF16)


def pair(get, first):
    return jnp.concatenate([get(first), get(first + 1)], axis=1)


def panel_kernel(meta, rb, C0, M0h, M0l, C1, M1h, M1l, X1h, X1l, gb, side):
    r = pl.program_id(0)
    p, q = meta[0], meta[1]
    i = r * PROW + p
    tiles = []
    for k in range(2):
        def get(a, k=k):
            whole = rb[:, k, a * ROWS + r]
            if k:
                order = [4 * zz + yy for zz in range(4) for yy in (1, 2, 3, 0)]
                whole = jnp.concatenate([whole[e : e + 1] for e in order], axis=0)
            return whole.reshape(N, RK)
        tiles += [pair(get, 0), pair(get, 2)]
    G0, G1, b0, b1 = solve(i, tiles, M0h, M0l, M1h, M1l, X1h, X1l)
    gb[0, :, 0:N] = b0
    gb[0, :, N : 2 * N] = b1

    def panel(k, C, G):
        a = lax.broadcasted_iota(jnp.int32, (N, N), 0)
        b = lax.broadcasted_iota(jnp.int32, (N, N), 1)
        pivots = jnp.sum(jnp.where(a == b, C[...], 0.0), axis=0, keepdims=True)

        @pl.when(i == k)
        def _():
            side[0] = C[...] * pivots

        @pl.when(i != k)
        def _():
            side[0] = G * pivots

    @pl.when(q == 0)
    def _():
        panel(0, C0, G0)

    @pl.when(q == 1)
    def _():
        panel(1, C1, G1)

    @pl.when(q > 1)
    def _():
        side[...] = jnp.zeros_like(side)


def final_kernel(
    rank, meta, shift, u, v, gb, side, rc, rsum, ksum,
    M0h, M0l, M1h, M1l, X1h, X1l, out, gcol, packed, D
):
    r = pl.program_id(0)
    p, q = meta[0], meta[1]

    @pl.when(r == 0)
    def _():
        for t in range(COLS):
            tiles = []
            for k in range(2):
                def get(a, k=k, t=t):
                    return jnp.concatenate(
                        [rc[s, k, 4 * t + a] for s in range(PROW)], axis=0
                    )
                tiles += [pair(get, 0), pair(get, 2)]
            _, _, b0, b1 = solve(q + PCOL * t, tiles, M0h, M0l, M1h, M1l, X1h, X1l)
            gcol[t, :, 0:N] = b0
            gcol[t, :, N : 2 * N] = b1

    i = r * PROW + p

    def put(t, value):
        for b in range(4):
            out[0, :, 4 * t + b, :] = value[:, 128 * b : 128 * b + 128]

    def trailing(t):
        j = q + PCOL * t
        U = jnp.concatenate([u[c, 0, t] for c in range(KIDS)], axis=1)
        V = jnp.concatenate([kept(v[c, 0, t], rank[c, r, t]) for c in range(KIDS)], axis=1)
        acc = nt(U, V) - nt(gb[0], gcol[t])
        put(t, jnp.where(i >= j, acc, 0.0))

        @pl.when(i == j)
        def _():
            for e in range(PROW):
                packed[KSLAB * e : KSLAB * e + KSLAB, :] = ksum[e, t]
            for e in range(PCOL):
                at = slice(RSLAB * e, RSLAB * e + RSLAB)
                packed[at, :] = packed[at, :] + rsum[e, t]
            unpack(D, packed, True)
            add_shift(D, shift[pl.ds(j, 1), :])
            put(t, acc + D[...])

    @pl.when(q > 1)
    def _():
        trailing(0)

    @pl.when(q <= 1)
    def _():
        put(0, side[0])

    trailing(1)


def total(values):
    return functools.reduce(lambda a, b: a + b, values)


def pick(flag, value):
    return jnp.where(flag, value, jnp.zeros_like(value))


def on_device(child_u, child_v, child_rank, diag_shift):
    p = lax.axis_index("prow")
    q = lax.axis_index("pcol")
    x, core = p // 2, p % 2
    z, y = q // 4, q % 4
    both = ("prow", "pcol")
    rank = child_rank[:, :, 0, :, 0]
    u = child_u[:, :, 0, :, 0]
    v = child_v[:, :, 0, :, 0]
    meta = jnp.stack([p, q, x, core]).astype(jnp.int32)

    sums = pl.pallas_call(
        column_kernel,
        out_shape=shape((PROW, COLS, KSLAB, 128), F32),
        in_specs=[SMEM, VMEM],
        out_specs=VMEM,
        scratch_shapes=[
            pltpu.VMEM((N, KIDS * ROWS * RK), BF16),
            pltpu.VMEM((PACK, 128), F32),
        ],
        compiler_params=params(32),
        cost_estimate=cost(3),
        name="column_sums",
    )(rank, v)
    parts = pl.pallas_call(
        pieces_kernel,
        out_shape=[shape((4, 4 * ROWS, 32, RK), BF16)] * 4
        + [shape((2, 4, 256, RK), BF16)]
        + [shape((8, 8, 64, RK), BF16)] * 2,
        in_specs=[SMEM, SMEM, VMEM, VMEM, pl.BlockSpec(memory_space=pl.ANY)],
        out_specs=[VMEM] * 7,
        scratch_shapes=[pltpu.VMEM((4 * ROWS, N, RK), BF16)],
        compiler_params=params(48),
        cost_estimate=cost(4),
        name="pieces",
    )(rank, meta, u, v, sums)
    raw, tile, cols = parts[:4], parts[4], parts[5:7]
    swap = [(i, i ^ 1) for i in range(8)]
    turn = [
        [(2 * a + c, 2 * ((a + s) % 4) + c) for a in range(4) for c in range(2)]
        for s in range(1, 4)
    ]
    down = [[(i, 4 * s + i) for i in range(4)] for s in range(1, 4)]

    kgot = lax.all_to_all(sums, "prow", 0, 0)
    tgot = [lax.ppermute(tile, both, [(PCOL, PCOL + s)]) for s in range(1, 4)]
    zgot = [lax.ppermute(raw[s], "pcol", [(k, 4 * s + k) for k in range(2)]) for s in range(1, 4)]
    kgot, tgot, zgot = lax.optimization_barrier((kgot, tgot, zgot))
    kslab = jnp.sum(kgot, axis=0)
    kall = lax.all_gather(kslab, "prow")

    got = [lax.ppermute(kslab[0], "pcol", [(0, s), (1, (1 + s) % 4)]) for s in range(1, 4)]
    tpay = pick((p == 1) & (q == 0), tile) + total(tgot)
    tgot = [
        lax.ppermute(tpay, both, [(PCOL + i, PCOL + 4 * s + i) for i in range(4)])
        for s in range(1, 4)
    ]
    got, tgot = lax.optimization_barrier((got, tgot))
    pay = [
        pick(y == k, kslab[0]) + total(pick((y + 4 - k) % 4 == s, got[s - 1]) for s in range(1, 4))
        for k in range(2)
    ]
    pay = pick(z == 0, jnp.concatenate(pay, axis=0))
    tpay = pick(z == 0, tpay) + total(tgot)

    got = [lax.ppermute(pay, "pcol", pairs) for pairs in down]
    thalf = lax.ppermute(tpay[0], "prow", [(1, 0)])
    hold = [
        pick(z == 0, raw[0][s]) + total(zgot[e][s] for e in range(3)) for s in range(4)
    ]
    ygot = [
        lax.ppermute(
            hold[s], "pcol", [(4 * a + k, 4 * a + (k + s) % 4) for a in range(4) for k in range(2)]
        )
        for s in range(1, 4)
    ]
    got, ygot, thalf, kall = lax.optimization_barrier((got, ygot, thalf, kall))
    pay = pay + total(got)
    thalf = jnp.where(core == 1, tpay[1], thalf)
    piece = jnp.stack(
        [
            pick(y == k, hold[0]) + total(pick((y + 4 - k) % 4 == s, ygot[s - 1]) for s in range(1, 4))
            for k in range(2)
        ]
    )
    rows_all = lax.all_gather(piece, "pcol")

    got = [lax.ppermute(pay, "prow", pairs) for pairs in turn]
    tgot = [
        lax.ppermute(thalf, "prow", [(c, 2 * s + c) for c in range(2)]) for s in range(1, 4)
    ]
    rsum = pl.pallas_call(
        row_kernel,
        out_shape=shape((PCOL, 4, RSLAB, 128), F32),
        in_specs=[SMEM, VMEM, pl.BlockSpec(memory_space=pl.ANY)],
        out_specs=VMEM,
        scratch_shapes=[pltpu.VMEM((N, 4 * RK), BF16)],
        compiler_params=params(32),
        cost_estimate=cost(4),
        name="row_sums",
    )(rank, u, kslab)
    got, tgot, rsum, cols, piece = lax.optimization_barrier((got, tgot, rsum, cols, piece))
    thalf = pick(x == 0, thalf) + total(tgot)
    tother = lax.ppermute(thalf, "prow", swap)

    own = jnp.stack([pay] + got)
    other = lax.ppermute(own, "prow", swap)
    arrived = [
        lax.ppermute(
            cols[h],
            both,
            [(a * PCOL + k, a * PCOL + a + 8 * (h ^ k)) for a in range(8) for k in range(2)],
        )
        for h in range(2)
    ]
    rparts = lax.all_to_all(rsum, "pcol", 0, 0)
    own, other, tother = lax.optimization_barrier((own, other, tother))

    square = shape((N, N), F32)
    narrow = shape((N, N), BF16)
    work = pltpu.VMEM((N, N), F32)
    C0, M0h, M0l, g01, A1 = pl.pallas_call(
        first_kernel,
        out_shape=[square, narrow, narrow, narrow, square],
        in_specs=[SMEM] + [VMEM] * 5,
        out_specs=[VMEM] * 5,
        scratch_shapes=[
            pltpu.VMEM((PACK, 128), F32),
            pltpu.VMEM((PACK, 128), F32),
            work,
            work,
            pltpu.VMEM((4, N, RK), BF16),
        ],
        compiler_params=params(32),
        cost_estimate=cost(28),
        name="first_pivot",
    )(meta, own, other, thalf, tother, diag_shift)
    arrived, rparts, A1 = lax.optimization_barrier((arrived, rparts, A1))
    side = q // 8
    hold = jnp.stack(
        [jnp.where(side == 0, arrived[k], arrived[1 - k]) for k in range(2)], axis=1
    )
    share = lax.all_to_all(hold, "prow", 0, 0)
    rown = jnp.sum(rparts, axis=0)
    rown = jnp.concatenate(
        [
            jnp.broadcast_to(jnp.stack([rown[h], rown[2 + h]]), (8, COLS, RSLAB, 128))
            for h in range(2)
        ],
        axis=0,
    )
    A1, hold, rown = lax.optimization_barrier((A1, hold, rown))
    C1, M1h, M1l, X1h, X1l = pl.pallas_call(
        second_kernel,
        out_shape=[square] + [narrow] * 4,
        in_specs=[VMEM] * 2,
        out_specs=[VMEM] * 5,
        scratch_shapes=[work, work],
        compiler_params=params(32),
        cost_estimate=cost(26),
        name="second_pivot",
    )(A1, g01)
    share, rown, rows_all, C1 = lax.optimization_barrier((share, rown, rows_all, C1))
    share = lax.dynamic_index_in_dim(share, q % PROW, 0, keepdims=False)
    cols_all = lax.all_gather(share, "prow")
    rall = lax.all_to_all(rown, "pcol", 0, 0)
    C1, share = lax.optimization_barrier((C1, share))
    gb, panels = pl.pallas_call(
        panel_kernel,
        grid=(ROWS,),
        out_shape=[shape((ROWS, N, 2 * N), BF16), shape((ROWS, N, N), F32)],
        in_specs=[SMEM] + [VMEM] * 9,
        out_specs=[
            pl.BlockSpec((1, N, 2 * N), lambda r: (r, 0, 0)),
            pl.BlockSpec((1, N, N), lambda r: (r, 0, 0)),
        ],
        compiler_params=params(48),
        cost_estimate=cost(17),
        name="panels",
    )(meta, rows_all, C0, M0h, M0l, C1, M1h, M1l, X1h, X1l)
    tiles = pl.BlockSpec((KIDS, 1, COLS, N, RK), lambda r: (0, r, 0, 0, 0))
    out = pl.pallas_call(
        final_kernel,
        grid=(ROWS,),
        out_shape=shape((ROWS, N, COLS * 4, 128), F32),
        in_specs=[
            SMEM,
            SMEM,
            VMEM,
            tiles,
            tiles,
            pl.BlockSpec((1, N, 2 * N), lambda r: (r, 0, 0)),
            pl.BlockSpec((1, N, N), lambda r: (r, 0, 0)),
        ]
        + [VMEM] * 9,
        out_specs=pl.BlockSpec((1, N, COLS * 4, 128), lambda r: (r, 0, 0, 0)),
        scratch_shapes=[
            pltpu.VMEM((COLS, N, 2 * N), BF16),
            pltpu.VMEM((PACK, 128), F32),
            pltpu.VMEM((N, N), F32),
        ],
        compiler_params=params(60),
        cost_estimate=cost(20),
        name="update",
    )(rank, meta, diag_shift, u, v, gb, panels, cols_all, rall, kall,
      M0h, M0l, M1h, M1l, X1h, X1l)
    return out.reshape(ROWS, 1, N, COLS, 1, N)


def solution(mesh):
    placed = (
        P(None, None, "prow", None, "pcol", None, None),
        P(None, None, "prow", None, "pcol", None, None),
        P(None, None, "prow", None, "pcol"),
        P(),
    )
    return jax.shard_map(
        on_device,
        mesh=mesh,
        in_specs=placed,
        out_specs=P(None, "prow", None, None, "pcol", None),
        check_vma=False,
    )
```

```python
import functools
import jax
import jax.numpy as jnp
from jax import lax
from jax.experimental import pallas as pl
from jax.experimental.pallas import tpu as pltpu
from jax.sharding import PartitionSpec as P

F32 = jnp.float32
BF16 = jnp.bfloat16
PROW, PCOL = 8, 16
ROWS, COLS, KIDS = 5, 2, 2
N, RK = 512, 128
TRI = [(a, b) for a in range(4) for b in range(a + 1)]
PACK = 128 * len(TRI)
KSLAB = PACK // PROW
RSLAB = PACK // PCOL
VMEM = pl.BlockSpec(memory_space=pltpu.VMEM)
SMEM = pl.BlockSpec(memory_space=pltpu.SMEM)
EXACT = lax.Precision.HIGHEST


def shape(dims, dtype):
    return jax.ShapeDtypeStruct(dims, dtype)


def cost(us):
    return pl.CostEstimate(flops=us * 1_000_000_000, transcendentals=0, bytes_accessed=1 << 20)


def params(mib):
    return pltpu.CompilerParams(vmem_limit_bytes=mib << 20)


def nt(a, b, precision=None):
    return lax.dot_general(
        a, b, (((1,), (1,)), ((), ())), precision=precision, preferred_element_type=F32
    )


def nn(a, b, precision=None):
    return lax.dot_general(
        a, b, (((1,), (0,)), ((), ())), precision=precision, preferred_element_type=F32
    )


def halves(x):
    hi = x.astype(BF16)
    return hi, (x - hi.astype(F32)).astype(BF16)


def kept(tile, rank):
    lane = lax.broadcasted_iota(jnp.int32, tile.shape, 1)
    return jnp.where(lane < rank, tile, jnp.zeros_like(tile))


def column_kernel(rank, v, out, cat, packed):
    for t in range(COLS):
        for c in range(KIDS):
            for r in range(ROWS):
                at = (c * ROWS + r) * RK
                cat[:, at : at + RK] = kept(v[c, r, t], rank[c, r, t])
        total = nt(cat[...], cat[...])
        for n, (a, b) in enumerate(TRI):
            packed[128 * n : 128 * n + 128, :] = total[
                128 * a : 128 * a + 128, 128 * b : 128 * b + 128
            ]
        for s in range(PROW):
            out[s, t] = packed[KSLAB * s : KSLAB * s + KSLAB, :]


def pieces_kernel(rank, meta, u, v, _, *refs):
    raw, tile, cols, masked = refs[:4], refs[4], refs[5:9], refs[9]
    root = jnp.where(meta[1] == 1, 1, 0)
    for c in range(KIDS):
        for r in range(ROWS):
            masked[c * ROWS + r] = kept(u[c, r, 0], rank[c, r, 0])
            masked[(KIDS + c) * ROWS + r] = kept(v[c, r, 0], rank[c, r, 0])
    for s in range(16):
        raw[s // 4][s % 4] = masked[:, 32 * s : 32 * s + 32, :]
    for s in range(8):
        part = slice(64 * s, 64 * s + 64)
        for a in range(2 * KIDS):
            tile[s // 4, a, 64 * (s % 4) : 64 * (s % 4) + 64, :] = masked[a * ROWS, part, :]
            for h in range(2):
                row = lax.rem(root + h, 2)
                to = cols[2 * h + s // 4]
                to[s % 4, a] = masked[a * ROWS + row, part, :]
                to[s % 4, 4 + a] = masked[a * ROWS + 2 + row, part, :]


def row_kernel(rank, u, _, rsum, cat):
    for r in range(4):
        for c in range(KIDS):
            for t in range(COLS):
                at = (2 * c + t) * RK
                cat[:, at : at + RK] = kept(u[c, r, t], rank[c, r, t])
        total = nt(cat[...], cat[...])
        for n, (a, b) in enumerate(TRI):
            for e in range(128 // 16):
                line = 128 * n + 16 * e
                rsum[line // RSLAB, r, line % RSLAB : line % RSLAB + 16, :] = total[
                    128 * a + 16 * e : 128 * a + 16 * e + 16, 128 * b : 128 * b + 128
                ]


def base_inverse(block):
    lane = lax.broadcasted_iota(jnp.int32, (8, 128), 1)
    sub = lax.broadcasted_iota(jnp.int32, (8, 128), 0)
    rows = [block[8 * v : 8 * v + 8, :] for v in range(16)]

    def wide(x):
        return jnp.broadcast_to(x, (8, 128))

    for J in range(16):
        inside = (lane >= 8 * J) & (lane < 8 * J + 8)
        B = [wide(rows[J][:, 8 * J + n : 8 * J + n + 1]) for n in range(8)]
        fwd = jnp.where(inside, jnp.where(lane - 8 * J == sub, 1.0, 0.0), rows[J])
        full = fwd
        roots = jnp.zeros((8, 128), F32)
        for k in range(8):
            r = lax.rsqrt(wide(B[k][k : k + 1, :]))
            row = wide(full[k : k + 1, :])
            mult = jnp.where(sub == k, 0.0, B[k] * (r * r))
            full = full - mult * row
            fwd = fwd - jnp.where(sub > k, mult, 0.0) * row
            for n in range(k + 1, 8):
                B[n] = B[n] - mult * wide(B[n][k : k + 1, :])
            roots = jnp.where(sub == k, r, roots)
        rows[J] = fwd * roots
        scaled = full * (roots * roots)
        Y = [wide(scaled[n : n + 1, :]) for n in range(8)]
        for v in range(J + 1, 16):
            b = [wide(rows[v][:, 8 * J + n : 8 * J + n + 1]) * Y[n] for n in range(8)]
            t = ((b[0] + b[1]) + (b[2] + b[3])) + ((b[4] + b[5]) + (b[6] + b[7]))
            rows[v] = jnp.where(inside, 0.0, rows[v]) - t
    return jnp.concatenate(
        [jnp.where(lane <= sub + 8 * v, rows[v], 0.0) for v in range(16)], axis=0
    )


def factor(A, C, M, steps):
    i = lax.broadcasted_iota(jnp.int32, (128, 128), 0)
    j = lax.broadcasted_iota(jnp.int32, (128, 128), 1)
    if steps[0] == 0:
        M[...] = jnp.zeros_like(M)
        C[...] = jnp.zeros_like(C)
    for b in steps:
        at = slice(128 * b, 128 * b + 128)
        inv = base_inverse(A[at, at])
        if b:
            left = nn(C[at, 0 : 128 * b], M[0 : 128 * b, 0 : 128 * b], EXACT)
            M[at, 0 : 128 * b] = -nn(inv, left, EXACT)
        M[at, at] = inv
        C[at, at] = jnp.where(i >= j, nt(A[at, at], inv, EXACT), 0.0)
        if b < 3:
            below = slice(128 * b + 128, N)
            panel = nt(A[below, at], inv, EXACT)
            C[below, at] = panel
            A[below, below] = A[below, below] - nt(panel, panel, EXACT)


def add_shift(A, line):
    i = lax.broadcasted_iota(jnp.int32, (N, N), 0)
    j = lax.broadcasted_iota(jnp.int32, (N, N), 1)
    A[...] = A[...] + jnp.where(i == j, line, 0.0)


def unpack(A, packed, mirror):
    for n, (a, b) in enumerate(TRI):
        block = packed[128 * n : 128 * n + 128, :]
        A[128 * a : 128 * a + 128, 128 * b : 128 * b + 128] = block
        if a != b:
            A[128 * b : 128 * b + 128, 128 * a : 128 * a + 128] = (
                block.T if mirror else jnp.zeros_like(block)
            )


def half_kernel(meta, own, other, shift, A, C, M, K1, packed):
    x, core = meta[2], meta[3]
    for s in range(4):
        chip = lax.rem(x - s + 4, 4)
        for part, lane in ((own, core), (other, 1 - core)):
            place = 2 * chip + lane
            at = pl.ds(pl.multiple_of(place * KSLAB, 8), KSLAB)
            packed[at, :] = part[s, 0:KSLAB, :]
            K1[at, :] = part[s, KSLAB : 2 * KSLAB, :]
    unpack(A, packed, False)
    add_shift(A, shift[0:1, :])
    factor(A, C, M, (0, 1))


def first_kernel(
    meta, A0, C0, M0, K1, town, tother, shift, C, Mh, Ml, Gb, A1, A, M, tile
):
    core = meta[3]
    for part, lane in ((town, core), (tother, 1 - core)):
        line = pl.multiple_of(lane * 256, 16)
        for a in range(4):
            tile[a, pl.ds(line, 256), :] = part[a]
    A[...] = A0[...]
    C[...] = C0[...]
    M[...] = M0[...]
    factor(A, C, M, (2, 3))
    hi, lo = halves(M[...])
    Mh[...] = hi
    Ml[...] = lo
    U = jnp.concatenate([tile[0], tile[1]], axis=1)
    V = jnp.concatenate([tile[2], tile[3]], axis=1)
    wh, wl = halves(nn(hi, V) + nn(lo, V))
    G = (nt(U, wh) + nt(U, wl)).astype(BF16)
    Gb[...] = G
    unpack(A, K1, False)
    add_shift(A, shift[1:2, :])
    A1[...] = A[...] + (nt(U, U) - nt(G, G))


def second_kernel(A1, Gb, C, Mh, Ml, Xh, Xl, A, M):
    A[...] = A1[...]
    factor(A, C, M, (0, 1, 2, 3))
    hi, lo = halves(M[...])
    Mh[...] = hi
    Ml[...] = lo
    xh, xl = halves(nn(hi, Gb[...]) + nn(lo, Gb[...]))
    Xh[...] = xh
    Xl[...] = xl


def solve(i, tiles, M0h, M0l, M1h, M1l, X1h, X1l):
    U0, V0, U1, V1 = tiles
    wh, wl = halves(nn(M0h[...], V0) + nn(M0l[...], V0))
    G0 = jnp.where(i > 0, nt(U0, wh) + nt(U0, wl), 0.0)
    b0 = G0.astype(BF16)
    wh, wl = halves(nn(M1h[...], V1) + nn(M1l[...], V1))
    G1 = (nt(U1, wh) + nt(U1, wl)) - (nt(b0, X1h[...]) + nt(b0, X1l[...]))
    G1 = jnp.where(i > 1, G1, 0.0)
    return G0, G1, b0, G1.astype(BF16)


def pair(get, first):
    return jnp.concatenate([get(first), get(first + 1)], axis=1)


def panel_kernel(meta, rb, C0, M0h, M0l, C1, M1h, M1l, X1h, X1l, gb, side):
    r = pl.program_id(0)
    p, q = meta[0], meta[1]
    i = r * PROW + p
    tiles = []
    for k in range(2):
        def get(a, k=k):
            whole = rb[:, k, a * ROWS + r]
            if k:
                order = [4 * zz + yy for zz in range(4) for yy in (1, 2, 3, 0)]
                whole = jnp.concatenate([whole[e : e + 1] for e in order], axis=0)
            return whole.reshape(N, RK)
        tiles += [pair(get, 0), pair(get, 2)]
    G0, G1, b0, b1 = solve(i, tiles, M0h, M0l, M1h, M1l, X1h, X1l)
    gb[0, :, 0:N] = b0
    gb[0, :, N : 2 * N] = b1

    def panel(k, C, G):
        a = lax.broadcasted_iota(jnp.int32, (N, N), 0)
        b = lax.broadcasted_iota(jnp.int32, (N, N), 1)
        pivots = jnp.sum(jnp.where(a == b, C[...], 0.0), axis=0, keepdims=True)

        @pl.when(i == k)
        def _():
            side[0] = C[...] * pivots

        @pl.when(i != k)
        def _():
            side[0] = G * pivots

    @pl.when(q == 0)
    def _():
        panel(0, C0, G0)

    @pl.when(q == 1)
    def _():
        panel(1, C1, G1)

    @pl.when(q > 1)
    def _():
        side[...] = jnp.zeros_like(side)


def final_kernel(
    rank, meta, shift, u, v, gb, side, rc, ksum,
    M0h, M0l, M1h, M1l, X1h, X1l, out, gcol, packed, D
):
    r = pl.program_id(0)
    p, q = meta[0], meta[1]
    home = lax.rem(q, PROW)

    @pl.when(r == 0)
    def _():
        for t in range(COLS):
            tiles = []
            for k in range(2):
                def get(a, k=k, t=t):
                    return jnp.concatenate(
                        [
                            rc[
                                2 * lax.rem(home // 2 + s, 4) + lax.rem(home + c, 2),
                                k,
                                4 * t + a,
                            ]
                            for c in range(2)
                            for s in range(4)
                        ],
                        axis=0,
                    )
                tiles += [pair(get, 0), pair(get, 2)]
            _, _, b0, b1 = solve(q + PCOL * t, tiles, M0h, M0l, M1h, M1l, X1h, X1l)
            gcol[t, :, 0:N] = b0
            gcol[t, :, N : 2 * N] = b1

    i = r * PROW + p

    def put(t, value):
        for b in range(4):
            out[0, :, 4 * t + b, :] = value[:, 128 * b : 128 * b + 128]

    def trailing(t):
        j = q + PCOL * t
        U = jnp.concatenate([u[c, 0, t] for c in range(KIDS)], axis=1)
        V = jnp.concatenate([kept(v[c, 0, t], rank[c, r, t]) for c in range(KIDS)], axis=1)
        acc = nt(U, V) - nt(gb[0], gcol[t])
        put(t, jnp.where(i >= j, acc, 0.0))

        @pl.when(i == j)
        def _():
            for e in range(PROW):
                packed[KSLAB * e : KSLAB * e + KSLAB, :] = ksum[e, t]
            unpack(D, packed, True)
            add_shift(D, shift[pl.ds(j, 1), :])
            put(t, acc + D[...])

    @pl.when(q > 1)
    def _():
        trailing(0)

    @pl.when(q <= 1)
    def _():
        put(0, side[0])

    trailing(1)


def diagonal_kernel(meta, rsum, old, out, packed, D):
    t = pl.program_id(0)
    out[...] = old[...]

    @pl.when((meta[0] == lax.rem(meta[1], PROW)) & (meta[1] + PCOL * t > 1))
    def _():
        for e in range(PCOL):
            packed[RSLAB * e : RSLAB * e + RSLAB, :] = rsum[e, t]
        unpack(D, packed, True)
        for k in range(COLS):
            @pl.when(t == k)
            def _():
                for b in range(4):
                    out[0, :, 4 * k + b, :] = (
                        out[0, :, 4 * k + b, :] + D[:, 128 * b : 128 * b + 128]
                    )


def total(values):
    return functools.reduce(lambda a, b: a + b, values)


def pick(flag, value):
    return jnp.where(flag, value, jnp.zeros_like(value))


def on_device(child_u, child_v, child_rank, diag_shift):
    p = lax.axis_index("prow")
    q = lax.axis_index("pcol")
    x, core = p // 2, p % 2
    z, y = q // 4, q % 4
    both = ("prow", "pcol")
    rank = child_rank[:, :, 0, :, 0]
    u = child_u[:, :, 0, :, 0]
    v = child_v[:, :, 0, :, 0]
    meta = jnp.stack([p, q, x, core]).astype(jnp.int32)

    sums = pl.pallas_call(
        column_kernel,
        out_shape=shape((PROW, COLS, KSLAB, 128), F32),
        in_specs=[SMEM, VMEM],
        out_specs=VMEM,
        scratch_shapes=[
            pltpu.VMEM((N, KIDS * ROWS * RK), BF16),
            pltpu.VMEM((PACK, 128), F32),
        ],
        compiler_params=params(32),
        cost_estimate=cost(3),
        name="column_sums",
    )(rank, v)
    parts = pl.pallas_call(
        pieces_kernel,
        out_shape=[shape((4, 4 * ROWS, 32, RK), BF16)] * 4
        + [shape((2, 4, 256, RK), BF16)]
        + [shape((4, 8, 64, RK), BF16)] * 4,
        in_specs=[SMEM, SMEM, VMEM, VMEM, pl.BlockSpec(memory_space=pl.ANY)],
        out_specs=[VMEM] * 9,
        scratch_shapes=[pltpu.VMEM((4 * ROWS, N, RK), BF16)],
        compiler_params=params(48),
        cost_estimate=cost(4),
        name="pieces",
    )(rank, meta, u, v, sums)
    raw, tile, cols = parts[:4], parts[4], parts[5:9]
    swap = [(i, i ^ 1) for i in range(8)]
    turn = [
        [(2 * a + c, 2 * ((a + s) % 4) + c) for a in range(4) for c in range(2)]
        for s in range(1, 4)
    ]
    down = [[(i, 4 * s + i) for i in range(4)] for s in range(1, 4)]

    kgot = lax.all_to_all(sums, "prow", 0, 0)
    tgot = [lax.ppermute(tile, both, [(PCOL, PCOL + s)]) for s in range(1, 4)]
    zgot = [lax.ppermute(raw[s], "pcol", [(k, 4 * s + k) for k in range(2)]) for s in range(1, 4)]
    kgot, tgot, zgot = lax.optimization_barrier((kgot, tgot, zgot))
    kslab = jnp.sum(kgot, axis=0)
    kall = lax.all_gather(kslab, "prow")

    got = [lax.ppermute(kslab[0], "pcol", [(0, s), (1, (1 + s) % 4)]) for s in range(1, 4)]
    tpay = pick((p == 1) & (q == 0), tile) + total(tgot)
    tgot = [
        lax.ppermute(tpay, both, [(PCOL + i, PCOL + 4 * s + i) for i in range(4)])
        for s in range(1, 4)
    ]
    got, tgot = lax.optimization_barrier((got, tgot))
    pay = [
        pick(y == k, kslab[0]) + total(pick((y + 4 - k) % 4 == s, got[s - 1]) for s in range(1, 4))
        for k in range(2)
    ]
    pay = pick(z == 0, jnp.concatenate(pay, axis=0))
    tpay = pick(z == 0, tpay) + total(tgot)

    got = [lax.ppermute(pay, "pcol", pairs) for pairs in down]
    thalf = lax.ppermute(tpay[0], "prow", [(1, 0)])
    hold = [
        pick(z == 0, raw[0][s]) + total(zgot[e][s] for e in range(3)) for s in range(4)
    ]
    ygot = [
        lax.ppermute(
            hold[s], "pcol", [(4 * a + k, 4 * a + (k + s) % 4) for a in range(4) for k in range(2)]
        )
        for s in range(1, 4)
    ]
    got, ygot, thalf, kall = lax.optimization_barrier((got, ygot, thalf, kall))
    pay = pay + total(got)
    thalf = jnp.where(core == 1, tpay[1], thalf)
    piece = jnp.stack(
        [
            pick(y == k, hold[0]) + total(pick((y + 4 - k) % 4 == s, ygot[s - 1]) for s in range(1, 4))
            for k in range(2)
        ]
    )
    rows_all = lax.all_gather(piece, "pcol")

    got = [lax.ppermute(pay, "prow", pairs) for pairs in turn]
    tgot = [
        lax.ppermute(thalf, "prow", [(c, 2 * s + c) for c in range(2)]) for s in range(1, 4)
    ]
    rsum = pl.pallas_call(
        row_kernel,
        out_shape=shape((PCOL, 4, RSLAB, 128), F32),
        in_specs=[SMEM, VMEM, pl.BlockSpec(memory_space=pl.ANY)],
        out_specs=VMEM,
        scratch_shapes=[pltpu.VMEM((N, 4 * RK), BF16)],
        compiler_params=params(32),
        cost_estimate=cost(4),
        name="row_sums",
    )(rank, u, kslab)
    got, tgot, rsum, cols, piece = lax.optimization_barrier((got, tgot, rsum, cols, piece))
    thalf = pick(x == 0, thalf) + total(tgot)
    tother = lax.ppermute(thalf, "prow", swap)

    own = jnp.stack([pay] + got)
    other = lax.ppermute(own, "prow", swap)
    arrived = [
        lax.ppermute(
            cols[2 * h + c],
            both,
            [
                (a * PCOL + k, (a ^ c) * PCOL + a + 8 * (h ^ k))
                for a in range(8)
                for k in range(2)
            ],
        )
        for h in range(2)
        for c in range(2)
    ]
    own, other, tother = lax.optimization_barrier((own, other, tother))

    square = shape((N, N), F32)
    narrow = shape((N, N), BF16)
    work = pltpu.VMEM((N, N), F32)
    A0, C0, M0, K1 = pl.pallas_call(
        half_kernel,
        out_shape=[square] * 3 + [shape((PACK, 128), F32)],
        in_specs=[SMEM] + [VMEM] * 3,
        out_specs=[VMEM] * 4,
        scratch_shapes=[pltpu.VMEM((PACK, 128), F32)],
        compiler_params=params(32),
        cost_estimate=cost(14),
        name="first_pivot_a",
    )(meta, own, other, diag_shift)
    C0, M0h, M0l, g01, A1 = pl.pallas_call(
        first_kernel,
        out_shape=[square, narrow, narrow, narrow, square],
        in_specs=[SMEM] + [VMEM] * 7,
        out_specs=[VMEM] * 5,
        scratch_shapes=[work, work, pltpu.VMEM((4, N, RK), BF16)],
        compiler_params=params(32),
        cost_estimate=cost(15),
        name="first_pivot_b",
    )(meta, A0, C0, M0, K1, thalf, tother, diag_shift)
    arrived, rsum, A1 = lax.optimization_barrier((arrived, rsum, A1))
    rparts = lax.all_to_all(rsum, "pcol", 0, 0)
    side = q // 8
    arrived = [arrived[0] + arrived[1], arrived[2] + arrived[3]]
    hold = jnp.stack(
        [jnp.where(side == 0, arrived[k], arrived[1 - k]) for k in range(2)], axis=1
    )
    lines = [
        [
            (a * PCOL + b, (a + 2 * s) % 8 * PCOL + b)
            for b in range(PCOL)
            for a in (b % 8 // 2 * 2, b % 8 // 2 * 2 + 1)
        ]
        for s in range(1, 4)
    ]
    sent = [lax.ppermute(hold[s], both, lines[s - 1]) for s in range(1, 4)]
    A1, hold = lax.optimization_barrier((A1, hold))
    C1, M1h, M1l, X1h, X1l = pl.pallas_call(
        second_kernel,
        out_shape=[square] + [narrow] * 4,
        in_specs=[VMEM] * 2,
        out_specs=[VMEM] * 5,
        scratch_shapes=[work, work],
        compiler_params=params(32),
        cost_estimate=cost(26),
        name="second_pivot",
    )(A1, g01)
    sent, rows_all, rparts, C1 = lax.optimization_barrier((sent, rows_all, rparts, C1))
    share = pick(x == (q % 8) // 2, hold[0]) + total(sent)
    cols_all = lax.all_gather(share, "prow")
    C1, share = lax.optimization_barrier((C1, share))
    rown = jnp.sum(rparts, axis=0)
    rown = jnp.concatenate(
        [
            jnp.broadcast_to(jnp.stack([rown[h], rown[2 + h]]), (8, COLS, RSLAB, 128))
            for h in range(2)
        ],
        axis=0,
    )
    rall = lax.all_to_all(rown, "pcol", 0, 0)
    C1, rown = lax.optimization_barrier((C1, rown))
    gb, panels = pl.pallas_call(
        panel_kernel,
        grid=(ROWS,),
        out_shape=[shape((ROWS, N, 2 * N), BF16), shape((ROWS, N, N), F32)],
        in_specs=[SMEM] + [VMEM] * 9,
        out_specs=[
            pl.BlockSpec((1, N, 2 * N), lambda r: (r, 0, 0)),
            pl.BlockSpec((1, N, N), lambda r: (r, 0, 0)),
        ],
        compiler_params=params(48),
        cost_estimate=cost(3),
        name="panels",
    )(meta, rows_all, C0, M0h, M0l, C1, M1h, M1l, X1h, X1l)
    tiles = pl.BlockSpec((KIDS, 1, COLS, N, RK), lambda r: (0, r, 0, 0, 0))
    out = pl.pallas_call(
        final_kernel,
        grid=(ROWS,),
        out_shape=shape((ROWS, N, COLS * 4, 128), F32),
        in_specs=[
            SMEM,
            SMEM,
            VMEM,
            tiles,
            tiles,
            pl.BlockSpec((1, N, 2 * N), lambda r: (r, 0, 0)),
            pl.BlockSpec((1, N, N), lambda r: (r, 0, 0)),
        ]
        + [VMEM] * 8,
        out_specs=pl.BlockSpec((1, N, COLS * 4, 128), lambda r: (r, 0, 0, 0)),
        scratch_shapes=[
            pltpu.VMEM((COLS, N, 2 * N), BF16),
            pltpu.VMEM((PACK, 128), F32),
            pltpu.VMEM((N, N), F32),
        ],
        compiler_params=params(60),
        cost_estimate=cost(20),
        name="update",
    )(rank, meta, diag_shift, u, v, gb, panels, cols_all, kall,
      M0h, M0l, M1h, M1l, X1h, X1l)
    block = pl.BlockSpec(
        (1, N, COLS * 4, 128), lambda t, meta: (2 * t + meta[1] // PROW, 0, 0, 0)
    )
    out = pl.pallas_call(
        diagonal_kernel,
        grid_spec=pltpu.PrefetchScalarGridSpec(
            num_scalar_prefetch=1,
            grid=(COLS,),
            in_specs=[VMEM, block],
            out_specs=block,
            scratch_shapes=[pltpu.VMEM((PACK, 128), F32), pltpu.VMEM((N, N), F32)],
        ),
        out_shape=shape((ROWS, N, COLS * 4, 128), F32),
        input_output_aliases={2: 0},
        compiler_params=params(32),
        cost_estimate=cost(4),
        name="diagonal",
    )(meta, rall, out)
    return out.reshape(ROWS, 1, N, COLS, 1, N)


def solution(mesh):
    placed = (
        P(None, None, "prow", None, "pcol", None, None),
        P(None, None, "prow", None, "pcol", None, None),
        P(None, None, "prow", None, "pcol"),
        P(),
    )
    return jax.shard_map(
        on_device,
        mesh=mesh,
        in_specs=placed,
        out_specs=P(None, "prow", None, None, "pcol", None),
        check_vma=False,
    )
```

```python
import functools
import jax
import jax.numpy as jnp
from jax import lax
from jax.experimental import pallas as pl
from jax.experimental.pallas import tpu as pltpu
from jax.sharding import PartitionSpec as P

F32 = jnp.float32
BF16 = jnp.bfloat16
PROW, PCOL = 8, 16
ROWS, COLS, KIDS = 5, 2, 2
N, RK = 512, 128
TRI = [(a, b) for a in range(4) for b in range(a + 1)]
PACK = 128 * len(TRI)
KSLAB = PACK // PROW
RSLAB = PACK // PCOL
VMEM = pl.BlockSpec(memory_space=pltpu.VMEM)
SMEM = pl.BlockSpec(memory_space=pltpu.SMEM)
EXACT = lax.Precision.HIGHEST


def shape(dims, dtype):
    return jax.ShapeDtypeStruct(dims, dtype)


def cost(us):
    return pl.CostEstimate(flops=us * 1_000_000_000, transcendentals=0, bytes_accessed=1 << 20)


def params(mib):
    return pltpu.CompilerParams(vmem_limit_bytes=mib << 20)


def nt(a, b, precision=None):
    return lax.dot_general(
        a, b, (((1,), (1,)), ((), ())), precision=precision, preferred_element_type=F32
    )


def nn(a, b, precision=None):
    return lax.dot_general(
        a, b, (((1,), (0,)), ((), ())), precision=precision, preferred_element_type=F32
    )


def halves(x):
    hi = x.astype(BF16)
    return hi, (x - hi.astype(F32)).astype(BF16)


def kept(tile, rank):
    lane = lax.broadcasted_iota(jnp.int32, tile.shape, 1)
    return jnp.where(lane < rank, tile, jnp.zeros_like(tile))


def column_kernel(rank, v, out, cat, packed):
    for t in range(COLS):
        for c in range(KIDS):
            for r in range(ROWS):
                at = (c * ROWS + r) * RK
                cat[:, at : at + RK] = kept(v[c, r, t], rank[c, r, t])
        total = nt(cat[...], cat[...])
        for n, (a, b) in enumerate(TRI):
            packed[128 * n : 128 * n + 128, :] = total[
                128 * a : 128 * a + 128, 128 * b : 128 * b + 128
            ]
        for s in range(PROW):
            out[s, t] = packed[KSLAB * s : KSLAB * s + KSLAB, :]


def pieces_kernel(rank, meta, u, v, _, *refs):
    raw, tile, cols, masked = refs[:4], refs[4], refs[5:9], refs[9]
    root = jnp.where(meta[1] == 1, 1, 0)
    for c in range(KIDS):
        for r in range(ROWS):
            masked[c * ROWS + r] = kept(u[c, r, 0], rank[c, r, 0])
            masked[(KIDS + c) * ROWS + r] = kept(v[c, r, 0], rank[c, r, 0])
    for s in range(16):
        raw[s // 4][s % 4] = masked[:, 32 * s : 32 * s + 32, :]
    for s in range(8):
        part = slice(64 * s, 64 * s + 64)
        for a in range(2 * KIDS):
            tile[s // 4, a, 64 * (s % 4) : 64 * (s % 4) + 64, :] = masked[a * ROWS, part, :]
            for h in range(2):
                row = lax.rem(root + h, 2)
                to = cols[2 * h + s // 4]
                to[s % 4, a] = masked[a * ROWS + row, part, :]
                to[s % 4, 4 + a] = masked[a * ROWS + 2 + row, part, :]


def row_kernel(rank, u, _, rsum, cat):
    for r in range(4):
        for c in range(KIDS):
            for t in range(COLS):
                at = (2 * c + t) * RK
                cat[:, at : at + RK] = kept(u[c, r, t], rank[c, r, t])
        total = nt(cat[...], cat[...])
        for n, (a, b) in enumerate(TRI):
            for e in range(128 // 16):
                line = 128 * n + 16 * e
                rsum[line // RSLAB, r, line % RSLAB : line % RSLAB + 16, :] = total[
                    128 * a + 16 * e : 128 * a + 16 * e + 16, 128 * b : 128 * b + 128
                ]


def base_inverse(block):
    lane = lax.broadcasted_iota(jnp.int32, (8, 128), 1)
    sub = lax.broadcasted_iota(jnp.int32, (8, 128), 0)
    rows = [block[8 * v : 8 * v + 8, :] for v in range(16)]

    def wide(x):
        return jnp.broadcast_to(x, (8, 128))

    for J in range(16):
        inside = (lane >= 8 * J) & (lane < 8 * J + 8)
        B = [wide(rows[J][:, 8 * J + n : 8 * J + n + 1]) for n in range(8)]
        fwd = jnp.where(inside, jnp.where(lane - 8 * J == sub, 1.0, 0.0), rows[J])
        full = fwd
        roots = jnp.zeros((8, 128), F32)
        for k in range(8):
            r = lax.rsqrt(wide(B[k][k : k + 1, :]))
            row = wide(full[k : k + 1, :])
            mult = jnp.where(sub == k, 0.0, B[k] * (r * r))
            full = full - mult * row
            fwd = fwd - jnp.where(sub > k, mult, 0.0) * row
            for n in range(k + 1, 8):
                B[n] = B[n] - mult * wide(B[n][k : k + 1, :])
            roots = jnp.where(sub == k, r, roots)
        rows[J] = fwd * roots
        scaled = full * (roots * roots)
        Y = [wide(scaled[n : n + 1, :]) for n in range(8)]
        for v in range(J + 1, 16):
            b = [wide(rows[v][:, 8 * J + n : 8 * J + n + 1]) * Y[n] for n in range(8)]
            t = ((b[0] + b[1]) + (b[2] + b[3])) + ((b[4] + b[5]) + (b[6] + b[7]))
            rows[v] = jnp.where(inside, 0.0, rows[v]) - t
    return jnp.concatenate(
        [jnp.where(lane <= sub + 8 * v, rows[v], 0.0) for v in range(16)], axis=0
    )


def factor(A, C, M, steps):
    i = lax.broadcasted_iota(jnp.int32, (128, 128), 0)
    j = lax.broadcasted_iota(jnp.int32, (128, 128), 1)
    if steps[0] == 0:
        M[...] = jnp.zeros_like(M)
        C[...] = jnp.zeros_like(C)
    for b in steps:
        at = slice(128 * b, 128 * b + 128)
        inv = base_inverse(A[at, at])
        if b:
            left = nn(C[at, 0 : 128 * b], M[0 : 128 * b, 0 : 128 * b], EXACT)
            M[at, 0 : 128 * b] = -nn(inv, left, EXACT)
        M[at, at] = inv
        C[at, at] = jnp.where(i >= j, nt(A[at, at], inv, EXACT), 0.0)
        if b < 3:
            below = slice(128 * b + 128, N)
            panel = nt(A[below, at], inv, EXACT)
            C[below, at] = panel
            A[below, below] = A[below, below] - nt(panel, panel, EXACT)


def add_shift(A, line):
    i = lax.broadcasted_iota(jnp.int32, (N, N), 0)
    j = lax.broadcasted_iota(jnp.int32, (N, N), 1)
    A[...] = A[...] + jnp.where(i == j, line, 0.0)


def unpack(A, packed, mirror):
    for n, (a, b) in enumerate(TRI):
        block = packed[128 * n : 128 * n + 128, :]
        A[128 * a : 128 * a + 128, 128 * b : 128 * b + 128] = block
        if a != b:
            A[128 * b : 128 * b + 128, 128 * a : 128 * a + 128] = (
                block.T if mirror else jnp.zeros_like(block)
            )


def half_kernel(meta, own, other, shift, A, C, M, K1, packed):
    x, core = meta[2], meta[3]
    for s in range(4):
        chip = lax.rem(x - s + 4, 4)
        for part, lane in ((own, core), (other, 1 - core)):
            place = 2 * chip + lane
            at = pl.ds(pl.multiple_of(place * KSLAB, 8), KSLAB)
            packed[at, :] = part[s, 0:KSLAB, :]
            K1[at, :] = part[s, KSLAB : 2 * KSLAB, :]
    unpack(A, packed, False)
    add_shift(A, shift[0:1, :])
    factor(A, C, M, (0, 1))


def first_kernel(
    meta, A0, C0, M0, K1, town, tother, shift, C, Mh, Ml, Gb, A1, A, M, tile
):
    core = meta[3]
    for part, lane in ((town, core), (tother, 1 - core)):
        line = pl.multiple_of(lane * 256, 16)
        for a in range(4):
            tile[a, pl.ds(line, 256), :] = part[a]
    A[...] = A0[...]
    C[...] = C0[...]
    M[...] = M0[...]
    factor(A, C, M, (2, 3))
    hi, lo = halves(M[...])
    Mh[...] = hi
    Ml[...] = lo
    U = jnp.concatenate([tile[0], tile[1]], axis=1)
    V = jnp.concatenate([tile[2], tile[3]], axis=1)
    wh, wl = halves(nn(hi, V) + nn(lo, V))
    G = (nt(U, wh) + nt(U, wl)).astype(BF16)
    Gb[...] = G
    unpack(A, K1, False)
    add_shift(A, shift[1:2, :])
    A1[...] = A[...] + (nt(U, U) - nt(G, G))


def second_kernel(A1, Gb, C, Mh, Ml, Xh, Xl, A, M):
    A[...] = A1[...]
    factor(A, C, M, (0, 1, 2, 3))
    hi, lo = halves(M[...])
    Mh[...] = hi
    Ml[...] = lo
    xh, xl = halves(nn(hi, Gb[...]) + nn(lo, Gb[...]))
    Xh[...] = xh
    Xl[...] = xl


def solve(i, tiles, M0h, M0l, M1h, M1l, X1h, X1l):
    U0, V0, U1, V1 = tiles
    wh, wl = halves(nn(M0h[...], V0) + nn(M0l[...], V0))
    G0 = jnp.where(i > 0, nt(U0, wh) + nt(U0, wl), 0.0)
    b0 = G0.astype(BF16)
    wh, wl = halves(nn(M1h[...], V1) + nn(M1l[...], V1))
    G1 = (nt(U1, wh) + nt(U1, wl)) - (nt(b0, X1h[...]) + nt(b0, X1l[...]))
    G1 = jnp.where(i > 1, G1, 0.0)
    return G0, G1, b0, G1.astype(BF16)


def pair(get, first):
    return jnp.concatenate([get(first), get(first + 1)], axis=1)


def panel_kernel(meta, rb, C0, M0h, M0l, C1, M1h, M1l, X1h, X1l, gb, side):
    r = pl.program_id(0)
    p, q = meta[0], meta[1]
    i = r * PROW + p
    tiles = []
    for k in range(2):
        def get(a, k=k):
            whole = rb[:, k, a * ROWS + r]
            if k:
                order = [4 * zz + yy for zz in range(4) for yy in (1, 2, 3, 0)]
                whole = jnp.concatenate([whole[e : e + 1] for e in order], axis=0)
            return whole.reshape(N, RK)
        tiles += [pair(get, 0), pair(get, 2)]
    G0, G1, b0, b1 = solve(i, tiles, M0h, M0l, M1h, M1l, X1h, X1l)
    gb[0, :, 0:N] = b0
    gb[0, :, N : 2 * N] = b1

    def panel(k, C, G):
        a = lax.broadcasted_iota(jnp.int32, (N, N), 0)
        b = lax.broadcasted_iota(jnp.int32, (N, N), 1)
        pivots = jnp.sum(jnp.where(a == b, C[...], 0.0), axis=0, keepdims=True)

        @pl.when(i == k)
        def _():
            side[0] = C[...] * pivots

        @pl.when(i != k)
        def _():
            side[0] = G * pivots

    @pl.when(q == 0)
    def _():
        panel(0, C0, G0)

    @pl.when(q == 1)
    def _():
        panel(1, C1, G1)

    @pl.when(q > 1)
    def _():
        side[...] = jnp.zeros_like(side)


def final_kernel(
    rank, meta, shift, u, v, gb, side, rc, ksum,
    M0h, M0l, M1h, M1l, X1h, X1l, out, gcol, packed, D
):
    r = pl.program_id(0)
    p, q = meta[0], meta[1]
    home = lax.rem(q, PROW)

    @pl.when(r == 0)
    def _():
        for t in range(COLS):
            tiles = []
            for k in range(2):
                def get(a, k=k, t=t):
                    return jnp.concatenate(
                        [
                            rc[
                                2 * lax.rem(home // 2 + s, 4) + lax.rem(home + c, 2),
                                k,
                                4 * t + a,
                            ]
                            for c in range(2)
                            for s in range(4)
                        ],
                        axis=0,
                    )
                tiles += [pair(get, 0), pair(get, 2)]
            _, _, b0, b1 = solve(q + PCOL * t, tiles, M0h, M0l, M1h, M1l, X1h, X1l)
            gcol[t, :, 0:N] = b0
            gcol[t, :, N : 2 * N] = b1

    i = r * PROW + p

    def put(t, value):
        for b in range(4):
            out[0, :, 4 * t + b, :] = value[:, 128 * b : 128 * b + 128]

    def trailing(t):
        j = q + PCOL * t
        U = jnp.concatenate([u[c, 0, t] for c in range(KIDS)], axis=1)
        V = jnp.concatenate([kept(v[c, 0, t], rank[c, r, t]) for c in range(KIDS)], axis=1)
        acc = nt(U, V) - nt(gb[0], gcol[t])
        put(t, jnp.where(i >= j, acc, 0.0))

        @pl.when(i == j)
        def _():
            for e in range(PROW):
                packed[KSLAB * e : KSLAB * e + KSLAB, :] = ksum[e, t]
            unpack(D, packed, True)
            add_shift(D, shift[pl.ds(j, 1), :])
            put(t, acc + D[...])

    @pl.when(q > 1)
    def _():
        trailing(0)

    @pl.when(q <= 1)
    def _():
        put(0, side[0])

    trailing(1)


def diagonal_kernel(meta, rsum, old, out, packed, D):
    t = pl.program_id(0)
    out[...] = old[...]

    @pl.when((meta[0] == lax.rem(meta[1], PROW)) & (meta[1] + PCOL * t > 1))
    def _():
        for e in range(PCOL):
            packed[RSLAB * e : RSLAB * e + RSLAB, :] = rsum[e, t]
        unpack(D, packed, True)
        for k in range(COLS):
            @pl.when(t == k)
            def _():
                for b in range(4):
                    out[0, :, 4 * k + b, :] = (
                        out[0, :, 4 * k + b, :] + D[:, 128 * b : 128 * b + 128]
                    )


def total(values):
    return functools.reduce(lambda a, b: a + b, values)


def pick(flag, value):
    return jnp.where(flag, value, jnp.zeros_like(value))


def on_device(child_u, child_v, child_rank, diag_shift):
    p = lax.axis_index("prow")
    q = lax.axis_index("pcol")
    x, core = p // 2, p % 2
    z, y = q // 4, q % 4
    both = ("prow", "pcol")
    rank = child_rank[:, :, 0, :, 0]
    u = child_u[:, :, 0, :, 0]
    v = child_v[:, :, 0, :, 0]
    meta = jnp.stack([p, q, x, core]).astype(jnp.int32)

    sums = pl.pallas_call(
        column_kernel,
        out_shape=shape((PROW, COLS, KSLAB, 128), F32),
        in_specs=[SMEM, VMEM],
        out_specs=VMEM,
        scratch_shapes=[
            pltpu.VMEM((N, KIDS * ROWS * RK), BF16),
            pltpu.VMEM((PACK, 128), F32),
        ],
        compiler_params=params(32),
        cost_estimate=cost(3),
        name="column_sums",
    )(rank, v)
    parts = pl.pallas_call(
        pieces_kernel,
        out_shape=[shape((4, 4 * ROWS, 32, RK), BF16)] * 4
        + [shape((2, 4, 256, RK), BF16)]
        + [shape((4, 8, 64, RK), BF16)] * 4,
        in_specs=[SMEM, SMEM, VMEM, VMEM, pl.BlockSpec(memory_space=pl.ANY)],
        out_specs=[VMEM] * 9,
        scratch_shapes=[pltpu.VMEM((4 * ROWS, N, RK), BF16)],
        compiler_params=params(48),
        cost_estimate=cost(4),
        name="pieces",
    )(rank, meta, u, v, sums)
    raw, tile, cols = parts[:4], parts[4], parts[5:9]
    swap = [(i, i ^ 1) for i in range(8)]
    turn = [
        [(2 * a + c, 2 * ((a + s) % 4) + c) for a in range(4) for c in range(2)]
        for s in range(1, 4)
    ]
    down = [[(i, 4 * s + i) for i in range(4)] for s in range(1, 4)]

    kgot = lax.all_to_all(sums, "prow", 0, 0)
    tgot = [lax.ppermute(tile, both, [(PCOL, PCOL + s)]) for s in range(1, 4)]
    zgot = [lax.ppermute(raw[s], "pcol", [(k, 4 * s + k) for k in range(2)]) for s in range(1, 4)]
    kgot, tgot, zgot = lax.optimization_barrier((kgot, tgot, zgot))
    kslab = jnp.sum(kgot, axis=0)
    kall = lax.all_gather(kslab, "prow")

    got = [lax.ppermute(kslab[0], "pcol", [(0, s), (1, (1 + s) % 4)]) for s in range(1, 4)]
    tpay = pick((p == 1) & (q == 0), tile) + total(tgot)
    tgot = [
        lax.ppermute(tpay, both, [(PCOL + i, PCOL + 4 * s + i) for i in range(4)])
        for s in range(1, 4)
    ]
    got, tgot = lax.optimization_barrier((got, tgot))
    pay = [
        pick(y == k, kslab[0]) + total(pick((y + 4 - k) % 4 == s, got[s - 1]) for s in range(1, 4))
        for k in range(2)
    ]
    pay = pick(z == 0, jnp.concatenate(pay, axis=0))
    tpay = pick(z == 0, tpay) + total(tgot)

    got = [lax.ppermute(pay, "pcol", pairs) for pairs in down]
    thalf = lax.ppermute(tpay[0], "prow", [(1, 0)])
    hold = [
        pick(z == 0, raw[0][s]) + total(zgot[e][s] for e in range(3)) for s in range(4)
    ]
    ygot = [
        lax.ppermute(
            hold[s], "pcol", [(4 * a + k, 4 * a + (k + s) % 4) for a in range(4) for k in range(2)]
        )
        for s in range(1, 4)
    ]
    got, ygot, thalf, kall = lax.optimization_barrier((got, ygot, thalf, kall))
    pay = pay + total(got)
    thalf = jnp.where(core == 1, tpay[1], thalf)
    piece = jnp.stack(
        [
            pick(y == k, hold[0]) + total(pick((y + 4 - k) % 4 == s, ygot[s - 1]) for s in range(1, 4))
            for k in range(2)
        ]
    )
    rows_all = lax.all_gather(piece, "pcol")

    got = [lax.ppermute(pay, "prow", pairs) for pairs in turn]
    tgot = [
        lax.ppermute(thalf, "prow", [(c, 2 * s + c) for c in range(2)]) for s in range(1, 4)
    ]
    rsum = pl.pallas_call(
        row_kernel,
        out_shape=shape((PCOL, 4, RSLAB, 128), F32),
        in_specs=[SMEM, VMEM, pl.BlockSpec(memory_space=pl.ANY)],
        out_specs=VMEM,
        scratch_shapes=[pltpu.VMEM((N, 4 * RK), BF16)],
        compiler_params=params(32),
        cost_estimate=cost(4),
        name="row_sums",
    )(rank, u, kslab)
    got, tgot, rsum, cols, piece = lax.optimization_barrier((got, tgot, rsum, cols, piece))
    thalf = pick(x == 0, thalf) + total(tgot)
    tother = lax.ppermute(thalf, "prow", swap)

    own = jnp.stack([pay] + got)
    other = lax.ppermute(own, "prow", swap)
    arrived = [
        lax.ppermute(
            cols[2 * h + c],
            both,
            [
                (a * PCOL + k, (a ^ c) * PCOL + a + 8 * (h ^ k))
                for a in range(8)
                for k in range(2)
            ],
        )
        for h in range(2)
        for c in range(2)
    ]
    own, other, tother = lax.optimization_barrier((own, other, tother))

    square = shape((N, N), F32)
    narrow = shape((N, N), BF16)
    work = pltpu.VMEM((N, N), F32)
    A0, C0, M0, K1 = pl.pallas_call(
        half_kernel,
        out_shape=[square] * 3 + [shape((PACK, 128), F32)],
        in_specs=[SMEM] + [VMEM] * 3,
        out_specs=[VMEM] * 4,
        scratch_shapes=[pltpu.VMEM((PACK, 128), F32)],
        compiler_params=params(32),
        cost_estimate=cost(14),
        name="first_pivot_a",
    )(meta, own, other, diag_shift)
    C0, M0h, M0l, g01, A1 = pl.pallas_call(
        first_kernel,
        out_shape=[square, narrow, narrow, narrow, square],
        in_specs=[SMEM] + [VMEM] * 7,
        out_specs=[VMEM] * 5,
        scratch_shapes=[work, work, pltpu.VMEM((4, N, RK), BF16)],
        compiler_params=params(32),
        cost_estimate=cost(15),
        name="first_pivot_b",
    )(meta, A0, C0, M0, K1, thalf, tother, diag_shift)
    arrived, rsum, A1 = lax.optimization_barrier((arrived, rsum, A1))
    rparts = lax.all_to_all(rsum, "pcol", 0, 0)
    side = q // 8
    arrived = [arrived[0] + arrived[1], arrived[2] + arrived[3]]
    hold = jnp.stack(
        [jnp.where(side == 0, arrived[k], arrived[1 - k]) for k in range(2)], axis=1
    )
    lines = [
        [
            (a * PCOL + b, (a + 2 * s) % 8 * PCOL + b)
            for b in range(PCOL)
            for a in (b % 8 // 2 * 2, b % 8 // 2 * 2 + 1)
        ]
        for s in range(1, 4)
    ]
    sent = [lax.ppermute(hold[s], both, lines[s - 1]) for s in range(1, 4)]
    A1, hold = lax.optimization_barrier((A1, hold))
    C1, M1h, M1l, X1h, X1l = pl.pallas_call(
        second_kernel,
        out_shape=[square] + [narrow] * 4,
        in_specs=[VMEM] * 2,
        out_specs=[VMEM] * 5,
        scratch_shapes=[work, work],
        compiler_params=params(32),
        cost_estimate=cost(26),
        name="second_pivot",
    )(A1, g01)
    sent, rows_all, rparts, C1 = lax.optimization_barrier((sent, rows_all, rparts, C1))
    share = pick(x == (q % 8) // 2, hold[0]) + total(sent)
    cols_all = lax.all_gather(share, "prow")
    C1, share = lax.optimization_barrier((C1, share))
    rown = jnp.sum(rparts, axis=0)
    rown = jnp.concatenate(
        [
            jnp.broadcast_to(jnp.stack([rown[h], rown[2 + h]]), (8, COLS, RSLAB, 128))
            for h in range(2)
        ],
        axis=0,
    )
    rall = lax.all_to_all(rown, "pcol", 0, 0)
    C1, rown = lax.optimization_barrier((C1, rown))
    whole = pl.BlockSpec((N, N), lambda r: (0, 0))
    gb, panels = pl.pallas_call(
        panel_kernel,
        grid=(ROWS,),
        out_shape=[shape((ROWS, N, 2 * N), BF16), shape((ROWS, N, N), F32)],
        in_specs=[SMEM, VMEM] + [whole] * 8,
        out_specs=[
            pl.BlockSpec((1, N, 2 * N), lambda r: (r, 0, 0)),
            pl.BlockSpec((1, N, N), lambda r: (r, 0, 0)),
        ],
        compiler_params=params(48),
        cost_estimate=cost(3),
        name="panels",
    )(meta, rows_all, C0, M0h, M0l, C1, M1h, M1l, X1h, X1l)
    tiles = pl.BlockSpec((KIDS, 1, COLS, N, RK), lambda r: (0, r, 0, 0, 0))
    out = pl.pallas_call(
        final_kernel,
        grid=(ROWS,),
        out_shape=shape((ROWS, N, COLS * 4, 128), F32),
        in_specs=[
            SMEM,
            SMEM,
            VMEM,
            tiles,
            tiles,
            pl.BlockSpec((1, N, 2 * N), lambda r: (r, 0, 0)),
            pl.BlockSpec((1, N, N), lambda r: (r, 0, 0)),
        ]
        + [VMEM] * 2
        + [whole] * 6,
        out_specs=pl.BlockSpec((1, N, COLS * 4, 128), lambda r: (r, 0, 0, 0)),
        scratch_shapes=[
            pltpu.VMEM((COLS, N, 2 * N), BF16),
            pltpu.VMEM((PACK, 128), F32),
            pltpu.VMEM((N, N), F32),
        ],
        compiler_params=params(60),
        cost_estimate=cost(20),
        name="update",
    )(rank, meta, diag_shift, u, v, gb, panels, cols_all, kall,
      M0h, M0l, M1h, M1l, X1h, X1l)
    block = pl.BlockSpec(
        (1, N, COLS * 4, 128), lambda t, meta: (2 * t + meta[1] // PROW, 0, 0, 0)
    )
    out = pl.pallas_call(
        diagonal_kernel,
        grid_spec=pltpu.PrefetchScalarGridSpec(
            num_scalar_prefetch=1,
            grid=(COLS,),
            in_specs=[VMEM, block],
            out_specs=block,
            scratch_shapes=[pltpu.VMEM((PACK, 128), F32), pltpu.VMEM((N, N), F32)],
        ),
        out_shape=shape((ROWS, N, COLS * 4, 128), F32),
        input_output_aliases={2: 0},
        compiler_params=params(32),
        cost_estimate=cost(4),
        name="diagonal",
    )(meta, rall, out)
    return out.reshape(ROWS, 1, N, COLS, 1, N)


def solution(mesh):
    placed = (
        P(None, None, "prow", None, "pcol", None, None),
        P(None, None, "prow", None, "pcol", None, None),
        P(None, None, "prow", None, "pcol"),
        P(),
    )
    return jax.shard_map(
        on_device,
        mesh=mesh,
        in_specs=placed,
        out_specs=P(None, "prow", None, None, "pcol", None),
        check_vma=False,
    )
```

```python
import functools
import jax
import jax.numpy as jnp
from jax import lax
from jax.experimental import pallas as pl
from jax.experimental.pallas import tpu as pltpu
from jax.sharding import PartitionSpec as P

F32 = jnp.float32
BF16 = jnp.bfloat16
PROW, PCOL = 8, 16
ROWS, COLS, KIDS = 5, 2, 2
N, RK = 512, 128
TRI = [(a, b) for a in range(4) for b in range(a + 1)]
PACK = 128 * len(TRI)
KSLAB = PACK // PROW
RSLAB = PACK // PCOL
VMEM = pl.BlockSpec(memory_space=pltpu.VMEM)
SMEM = pl.BlockSpec(memory_space=pltpu.SMEM)
EXACT = lax.Precision.HIGHEST


def shape(dims, dtype):
    return jax.ShapeDtypeStruct(dims, dtype)


def cost(us):
    return pl.CostEstimate(flops=us * 1_000_000_000, transcendentals=0, bytes_accessed=1 << 20)


def params(mib):
    return pltpu.CompilerParams(vmem_limit_bytes=mib << 20)


def nt(a, b, precision=None):
    return lax.dot_general(
        a, b, (((1,), (1,)), ((), ())), precision=precision, preferred_element_type=F32
    )


def nn(a, b, precision=None):
    return lax.dot_general(
        a, b, (((1,), (0,)), ((), ())), precision=precision, preferred_element_type=F32
    )


def halves(x):
    hi = x.astype(BF16)
    return hi, (x - hi.astype(F32)).astype(BF16)


def kept(tile, rank):
    lane = lax.broadcasted_iota(jnp.int32, tile.shape, 1)
    return jnp.where(lane < rank, tile, jnp.zeros_like(tile))


def column_kernel(rank, v, out, cat, packed):
    for t in range(COLS):
        for c in range(KIDS):
            for r in range(ROWS):
                at = (c * ROWS + r) * RK
                cat[:, at : at + RK] = kept(v[c, r, t], rank[c, r, t])
        total = nt(cat[...], cat[...])
        for n, (a, b) in enumerate(TRI):
            packed[128 * n : 128 * n + 128, :] = total[
                128 * a : 128 * a + 128, 128 * b : 128 * b + 128
            ]
        for s in range(PROW):
            out[s, t] = packed[KSLAB * s : KSLAB * s + KSLAB, :]


def pieces_kernel(rank, meta, u, v, _, *refs):
    raw, tile, cols, masked = refs[:4], refs[4], refs[5:9], refs[9]
    root = jnp.where(meta[1] == 1, 1, 0)
    for c in range(KIDS):
        for r in range(ROWS):
            masked[c * ROWS + r] = kept(u[c, r, 0], rank[c, r, 0])
            masked[(KIDS + c) * ROWS + r] = kept(v[c, r, 0], rank[c, r, 0])
    for s in range(16):
        raw[s // 4][s % 4] = masked[:, 32 * s : 32 * s + 32, :]
    for s in range(8):
        part = slice(64 * s, 64 * s + 64)
        for a in range(2 * KIDS):
            tile[s // 4, a, 64 * (s % 4) : 64 * (s % 4) + 64, :] = masked[a * ROWS, part, :]
            for h in range(2):
                row = lax.rem(root + h, 2)
                to = cols[2 * h + s // 4]
                to[s % 4, a] = masked[a * ROWS + row, part, :]
                to[s % 4, 4 + a] = masked[a * ROWS + 2 + row, part, :]


def row_kernel(rank, u, _, rsum, cat):
    for r in range(4):
        for c in range(KIDS):
            for t in range(COLS):
                at = (2 * c + t) * RK
                cat[:, at : at + RK] = kept(u[c, r, t], rank[c, r, t])
        total = nt(cat[...], cat[...])
        for n, (a, b) in enumerate(TRI):
            for e in range(128 // 16):
                line = 128 * n + 16 * e
                rsum[line // RSLAB, r, line % RSLAB : line % RSLAB + 16, :] = total[
                    128 * a + 16 * e : 128 * a + 16 * e + 16, 128 * b : 128 * b + 128
                ]


def base_inverse(block):
    lane = lax.broadcasted_iota(jnp.int32, (8, 128), 1)
    sub = lax.broadcasted_iota(jnp.int32, (8, 128), 0)
    rows = [block[8 * v : 8 * v + 8, :] for v in range(16)]

    def wide(x):
        return jnp.broadcast_to(x, (8, 128))

    for J in range(16):
        inside = (lane >= 8 * J) & (lane < 8 * J + 8)
        B = [wide(rows[J][:, 8 * J + n : 8 * J + n + 1]) for n in range(8)]
        fwd = jnp.where(inside, jnp.where(lane - 8 * J == sub, 1.0, 0.0), rows[J])
        full = fwd
        roots = jnp.zeros((8, 128), F32)
        for k in range(8):
            r = lax.rsqrt(wide(B[k][k : k + 1, :]))
            row = wide(full[k : k + 1, :])
            mult = jnp.where(sub == k, 0.0, B[k] * (r * r))
            full = full - mult * row
            fwd = fwd - jnp.where(sub > k, mult, 0.0) * row
            for n in range(k + 1, 8):
                B[n] = B[n] - mult * wide(B[n][k : k + 1, :])
            roots = jnp.where(sub == k, r, roots)
        rows[J] = fwd * roots
        scaled = full * (roots * roots)
        Y = [wide(scaled[n : n + 1, :]) for n in range(8)]
        for v in range(J + 1, 16):
            b = [wide(rows[v][:, 8 * J + n : 8 * J + n + 1]) * Y[n] for n in range(8)]
            t = ((b[0] + b[1]) + (b[2] + b[3])) + ((b[4] + b[5]) + (b[6] + b[7]))
            rows[v] = jnp.where(inside, 0.0, rows[v]) - t
    return jnp.concatenate(
        [jnp.where(lane <= sub + 8 * v, rows[v], 0.0) for v in range(16)], axis=0
    )


def factor(A, C, M, steps):
    i = lax.broadcasted_iota(jnp.int32, (128, 128), 0)
    j = lax.broadcasted_iota(jnp.int32, (128, 128), 1)
    if steps[0] == 0:
        M[...] = jnp.zeros_like(M)
        C[...] = jnp.zeros_like(C)
    for b in steps:
        at = slice(128 * b, 128 * b + 128)
        inv = base_inverse(A[at, at])
        if b:
            left = nn(C[at, 0 : 128 * b], M[0 : 128 * b, 0 : 128 * b], EXACT)
            M[at, 0 : 128 * b] = -nn(inv, left, EXACT)
        M[at, at] = inv
        C[at, at] = jnp.where(i >= j, nt(A[at, at], inv, EXACT), 0.0)
        if b < 3:
            below = slice(128 * b + 128, N)
            panel = nt(A[below, at], inv, EXACT)
            C[below, at] = panel
            A[below, below] = A[below, below] - nt(panel, panel, EXACT)


def add_shift(A, line):
    i = lax.broadcasted_iota(jnp.int32, (N, N), 0)
    j = lax.broadcasted_iota(jnp.int32, (N, N), 1)
    A[...] = A[...] + jnp.where(i == j, line, 0.0)


def unpack(A, packed, mirror):
    for n, (a, b) in enumerate(TRI):
        block = packed[128 * n : 128 * n + 128, :]
        A[128 * a : 128 * a + 128, 128 * b : 128 * b + 128] = block
        if a != b:
            A[128 * b : 128 * b + 128, 128 * a : 128 * a + 128] = (
                block.T if mirror else jnp.zeros_like(block)
            )


def half_kernel(meta, own, other, shift, A, C, M, K1, packed):
    x, core = meta[2], meta[3]
    for s in range(4):
        chip = lax.rem(x - s + 4, 4)
        for part, lane in ((own, core), (other, 1 - core)):
            place = 2 * chip + lane
            at = pl.ds(pl.multiple_of(place * KSLAB, 8), KSLAB)
            packed[at, :] = part[s, 0:KSLAB, :]
            K1[at, :] = part[s, KSLAB : 2 * KSLAB, :]
    unpack(A, packed, False)
    add_shift(A, shift[0:1, :])
    factor(A, C, M, (0, 1))


def first_kernel(
    meta, A0, C0, M0, K1, town, tother, shift, C, Mh, Ml, Gb, A1, A, M, tile
):
    core = meta[3]
    for part, lane in ((town, core), (tother, 1 - core)):
        line = pl.multiple_of(lane * 256, 16)
        for a in range(4):
            tile[a, pl.ds(line, 256), :] = part[a]
    A[...] = A0[...]
    C[...] = C0[...]
    M[...] = M0[...]
    factor(A, C, M, (2, 3))
    hi, lo = halves(M[...])
    Mh[...] = hi
    Ml[...] = lo
    U = jnp.concatenate([tile[0], tile[1]], axis=1)
    V = jnp.concatenate([tile[2], tile[3]], axis=1)
    wh, wl = halves(nn(hi, V) + nn(lo, V))
    G = (nt(U, wh) + nt(U, wl)).astype(BF16)
    Gb[...] = G
    unpack(A, K1, False)
    add_shift(A, shift[1:2, :])
    A1[...] = A[...] + (nt(U, U) - nt(G, G))


def second_kernel(A1, Gb, C, Mh, Ml, Xh, Xl, A, M):
    A[...] = A1[...]
    factor(A, C, M, (0, 1, 2, 3))
    hi, lo = halves(M[...])
    Mh[...] = hi
    Ml[...] = lo
    xh, xl = halves(nn(hi, Gb[...]) + nn(lo, Gb[...]))
    Xh[...] = xh
    Xl[...] = xl


def solve(i, tiles, M0h, M0l, M1h, M1l, X1h, X1l):
    U0, V0, U1, V1 = tiles
    wh, wl = halves(nn(M0h[...], V0) + nn(M0l[...], V0))
    left = jnp.concatenate([U0, U0], axis=1)
    G0 = jnp.where(i > 0, nt(left, jnp.concatenate([wh, wl], axis=1)), 0.0)
    b0 = G0.astype(BF16)
    wh, wl = halves(nn(M1h[...], V1) + nn(M1l[...], V1))
    left = jnp.concatenate([U1, U1, -b0, -b0], axis=1)
    G1 = nt(left, jnp.concatenate([wh, wl, X1h[...], X1l[...]], axis=1))
    G1 = jnp.where(i > 1, G1, 0.0)
    return G0, G1, b0, G1.astype(BF16)


def pair(get, first):
    return jnp.concatenate([get(first), get(first + 1)], axis=1)


def panel_kernel(meta, rb, C0, M0h, M0l, C1, M1h, M1l, X1h, X1l, gb, side):
    r = pl.program_id(0)
    p, q = meta[0], meta[1]
    i = r * PROW + p
    tiles = []
    for k in range(2):
        def get(a, k=k):
            whole = rb[:, k, a * ROWS + r]
            if k:
                order = [4 * zz + yy for zz in range(4) for yy in (1, 2, 3, 0)]
                whole = jnp.concatenate([whole[e : e + 1] for e in order], axis=0)
            return whole.reshape(N, RK)
        tiles += [pair(get, 0), pair(get, 2)]
    G0, G1, b0, b1 = solve(i, tiles, M0h, M0l, M1h, M1l, X1h, X1l)
    gb[0, :, 0:N] = b0
    gb[0, :, N : 2 * N] = b1

    def panel(k, C, G):
        a = lax.broadcasted_iota(jnp.int32, (N, N), 0)
        b = lax.broadcasted_iota(jnp.int32, (N, N), 1)
        pivots = jnp.sum(jnp.where(a == b, C[...], 0.0), axis=0, keepdims=True)

        @pl.when(i == k)
        def _():
            side[0] = C[...] * pivots

        @pl.when(i != k)
        def _():
            side[0] = G * pivots

    @pl.when(q == 0)
    def _():
        panel(0, C0, G0)

    @pl.when(q == 1)
    def _():
        panel(1, C1, G1)

    @pl.when(q > 1)
    def _():
        side[...] = jnp.zeros_like(side)


def final_kernel(
    rank, meta, shift, u, v, gb, side, rc, ksum,
    M0h, M0l, M1h, M1l, X1h, X1l, out, gcol, packed, D
):
    r = pl.program_id(0)
    p, q = meta[0], meta[1]
    home = lax.rem(q, PROW)

    @pl.when(r == 0)
    def _():
        for t in range(COLS):
            tiles = []
            for k in range(2):
                def get(a, k=k, t=t):
                    return jnp.concatenate(
                        [
                            rc[
                                2 * lax.rem(home // 2 + s, 4) + lax.rem(home + c, 2),
                                k,
                                4 * t + a,
                            ]
                            for c in range(2)
                            for s in range(4)
                        ],
                        axis=0,
                    )
                tiles += [pair(get, 0), pair(get, 2)]
            _, _, b0, b1 = solve(q + PCOL * t, tiles, M0h, M0l, M1h, M1l, X1h, X1l)
            gcol[t, :, 0:N] = b0
            gcol[t, :, N : 2 * N] = b1

    i = r * PROW + p

    def put(t, value):
        for b in range(4):
            out[0, :, 4 * t + b, :] = value[:, 128 * b : 128 * b + 128]

    def trailing(t):
        j = q + PCOL * t
        U = jnp.concatenate([u[c, 0, t] for c in range(KIDS)], axis=1)
        V = jnp.concatenate([kept(v[c, 0, t], rank[c, r, t]) for c in range(KIDS)], axis=1)
        acc = nt(U, V) - nt(gb[0], gcol[t])
        put(t, jnp.where(i >= j, acc, 0.0))

        @pl.when(i == j)
        def _():
            for e in range(PROW):
                packed[KSLAB * e : KSLAB * e + KSLAB, :] = ksum[e, t]
            unpack(D, packed, True)
            add_shift(D, shift[pl.ds(j, 1), :])
            put(t, acc + D[...])

    @pl.when(q > 1)
    def _():
        trailing(0)

    @pl.when(q <= 1)
    def _():
        put(0, side[0])

    trailing(1)


def diagonal_kernel(meta, rsum, old, out, packed, D):
    t = pl.program_id(0)
    out[...] = old[...]

    @pl.when((meta[0] == lax.rem(meta[1], PROW)) & (meta[1] + PCOL * t > 1))
    def _():
        for e in range(PCOL):
            packed[RSLAB * e : RSLAB * e + RSLAB, :] = rsum[e, t]
        unpack(D, packed, True)
        for k in range(COLS):
            @pl.when(t == k)
            def _():
                for b in range(4):
                    out[0, :, 4 * k + b, :] = (
                        out[0, :, 4 * k + b, :] + D[:, 128 * b : 128 * b + 128]
                    )


def total(values):
    return functools.reduce(lambda a, b: a + b, values)


def pick(flag, value):
    return jnp.where(flag, value, jnp.zeros_like(value))


def on_device(child_u, child_v, child_rank, diag_shift):
    p = lax.axis_index("prow")
    q = lax.axis_index("pcol")
    x, core = p // 2, p % 2
    z, y = q // 4, q % 4
    both = ("prow", "pcol")
    rank = child_rank[:, :, 0, :, 0]
    u = child_u[:, :, 0, :, 0]
    v = child_v[:, :, 0, :, 0]
    meta = jnp.stack([p, q, x, core]).astype(jnp.int32)

    sums = pl.pallas_call(
        column_kernel,
        out_shape=shape((PROW, COLS, KSLAB, 128), F32),
        in_specs=[SMEM, VMEM],
        out_specs=VMEM,
        scratch_shapes=[
            pltpu.VMEM((N, KIDS * ROWS * RK), BF16),
            pltpu.VMEM((PACK, 128), F32),
        ],
        compiler_params=params(32),
        cost_estimate=cost(3),
        name="column_sums",
    )(rank, v)
    parts = pl.pallas_call(
        pieces_kernel,
        out_shape=[shape((4, 4 * ROWS, 32, RK), BF16)] * 4
        + [shape((2, 4, 256, RK), BF16)]
        + [shape((4, 8, 64, RK), BF16)] * 4,
        in_specs=[SMEM, SMEM, VMEM, VMEM, pl.BlockSpec(memory_space=pl.ANY)],
        out_specs=[VMEM] * 9,
        scratch_shapes=[pltpu.VMEM((4 * ROWS, N, RK), BF16)],
        compiler_params=params(48),
        cost_estimate=cost(4),
        name="pieces",
    )(rank, meta, u, v, sums)
    raw, tile, cols = parts[:4], parts[4], parts[5:9]
    swap = [(i, i ^ 1) for i in range(8)]
    turn = [
        [(2 * a + c, 2 * ((a + s) % 4) + c) for a in range(4) for c in range(2)]
        for s in range(1, 4)
    ]
    down = [[(i, 4 * s + i) for i in range(4)] for s in range(1, 4)]

    kgot = lax.all_to_all(sums, "prow", 0, 0)
    tgot = [lax.ppermute(tile, both, [(PCOL, PCOL + s)]) for s in range(1, 4)]
    zgot = [lax.ppermute(raw[s], "pcol", [(k, 4 * s + k) for k in range(2)]) for s in range(1, 4)]
    kgot, tgot, zgot = lax.optimization_barrier((kgot, tgot, zgot))
    kslab = jnp.sum(kgot, axis=0)
    kall = lax.all_gather(kslab, "prow")

    got = [lax.ppermute(kslab[0], "pcol", [(0, s), (1, (1 + s) % 4)]) for s in range(1, 4)]
    tpay = pick((p == 1) & (q == 0), tile) + total(tgot)
    tgot = [
        lax.ppermute(tpay, both, [(PCOL + i, PCOL + 4 * s + i) for i in range(4)])
        for s in range(1, 4)
    ]
    got, tgot = lax.optimization_barrier((got, tgot))
    pay = [
        pick(y == k, kslab[0]) + total(pick((y + 4 - k) % 4 == s, got[s - 1]) for s in range(1, 4))
        for k in range(2)
    ]
    pay = pick(z == 0, jnp.concatenate(pay, axis=0))
    tpay = pick(z == 0, tpay) + total(tgot)

    got = [lax.ppermute(pay, "pcol", pairs) for pairs in down]
    thalf = lax.ppermute(tpay[0], "prow", [(1, 0)])
    hold = [
        pick(z == 0, raw[0][s]) + total(zgot[e][s] for e in range(3)) for s in range(4)
    ]
    ygot = [
        lax.ppermute(
            hold[s], "pcol", [(4 * a + k, 4 * a + (k + s) % 4) for a in range(4) for k in range(2)]
        )
        for s in range(1, 4)
    ]
    got, ygot, thalf, kall = lax.optimization_barrier((got, ygot, thalf, kall))
    pay = pay + total(got)
    thalf = jnp.where(core == 1, tpay[1], thalf)
    piece = jnp.stack(
        [
            pick(y == k, hold[0]) + total(pick((y + 4 - k) % 4 == s, ygot[s - 1]) for s in range(1, 4))
            for k in range(2)
        ]
    )
    rows_all = lax.all_gather(piece, "pcol")

    got = [lax.ppermute(pay, "prow", pairs) for pairs in turn]
    tgot = [
        lax.ppermute(thalf, "prow", [(c, 2 * s + c) for c in range(2)]) for s in range(1, 4)
    ]
    rsum = pl.pallas_call(
        row_kernel,
        out_shape=shape((PCOL, 4, RSLAB, 128), F32),
        in_specs=[SMEM, VMEM, pl.BlockSpec(memory_space=pl.ANY)],
        out_specs=VMEM,
        scratch_shapes=[pltpu.VMEM((N, 4 * RK), BF16)],
        compiler_params=params(32),
        cost_estimate=cost(4),
        name="row_sums",
    )(rank, u, kslab)
    got, tgot, rsum, cols, piece = lax.optimization_barrier((got, tgot, rsum, cols, piece))
    thalf = pick(x == 0, thalf) + total(tgot)
    tother = lax.ppermute(thalf, "prow", swap)

    own = jnp.stack([pay] + got)
    other = lax.ppermute(own, "prow", swap)
    arrived = [
        lax.ppermute(
            cols[2 * h + c],
            both,
            [
                (a * PCOL + k, (a ^ c) * PCOL + a + 8 * (h ^ k))
                for a in range(8)
                for k in range(2)
            ],
        )
        for h in range(2)
        for c in range(2)
    ]
    own, other, tother = lax.optimization_barrier((own, other, tother))

    square = shape((N, N), F32)
    narrow = shape((N, N), BF16)
    work = pltpu.VMEM((N, N), F32)
    A0, C0, M0, K1 = pl.pallas_call(
        half_kernel,
        out_shape=[square] * 3 + [shape((PACK, 128), F32)],
        in_specs=[SMEM] + [VMEM] * 3,
        out_specs=[VMEM] * 4,
        scratch_shapes=[pltpu.VMEM((PACK, 128), F32)],
        compiler_params=params(32),
        cost_estimate=cost(14),
        name="first_pivot_a",
    )(meta, own, other, diag_shift)
    C0, M0h, M0l, g01, A1 = pl.pallas_call(
        first_kernel,
        out_shape=[square, narrow, narrow, narrow, square],
        in_specs=[SMEM] + [VMEM] * 7,
        out_specs=[VMEM] * 5,
        scratch_shapes=[work, work, pltpu.VMEM((4, N, RK), BF16)],
        compiler_params=params(32),
        cost_estimate=cost(15),
        name="first_pivot_b",
    )(meta, A0, C0, M0, K1, thalf, tother, diag_shift)
    arrived, rsum, A1 = lax.optimization_barrier((arrived, rsum, A1))
    rparts = lax.all_to_all(rsum, "pcol", 0, 0)
    side = q // 8
    arrived = [arrived[0] + arrived[1], arrived[2] + arrived[3]]
    hold = jnp.stack(
        [jnp.where(side == 0, arrived[k], arrived[1 - k]) for k in range(2)], axis=1
    )
    lines = [
        [
            (a * PCOL + b, (a + 2 * s) % 8 * PCOL + b)
            for b in range(PCOL)
            for a in (b % 8 // 2 * 2, b % 8 // 2 * 2 + 1)
        ]
        for s in range(1, 4)
    ]
    sent = [lax.ppermute(hold[s], both, lines[s - 1]) for s in range(1, 4)]
    A1, hold = lax.optimization_barrier((A1, hold))
    C1, M1h, M1l, X1h, X1l = pl.pallas_call(
        second_kernel,
        out_shape=[square] + [narrow] * 4,
        in_specs=[VMEM] * 2,
        out_specs=[VMEM] * 5,
        scratch_shapes=[work, work],
        compiler_params=params(32),
        cost_estimate=cost(26),
        name="second_pivot",
    )(A1, g01)
    sent, rows_all, rparts, C1 = lax.optimization_barrier((sent, rows_all, rparts, C1))
    share = pick(x == (q % 8) // 2, hold[0]) + total(sent)
    cols_all = lax.all_gather(share, "prow")
    C1, share = lax.optimization_barrier((C1, share))
    rown = jnp.sum(rparts, axis=0)
    rown = jnp.concatenate(
        [
            jnp.broadcast_to(jnp.stack([rown[h], rown[2 + h]]), (8, COLS, RSLAB, 128))
            for h in range(2)
        ],
        axis=0,
    )
    rall = lax.all_to_all(rown, "pcol", 0, 0)
    C1, rown = lax.optimization_barrier((C1, rown))
    whole = pl.BlockSpec((N, N), lambda r: (0, 0))
    gb, panels = pl.pallas_call(
        panel_kernel,
        grid=(ROWS,),
        out_shape=[shape((ROWS, N, 2 * N), BF16), shape((ROWS, N, N), F32)],
        in_specs=[SMEM, VMEM] + [whole] * 8,
        out_specs=[
            pl.BlockSpec((1, N, 2 * N), lambda r: (r, 0, 0)),
            pl.BlockSpec((1, N, N), lambda r: (r, 0, 0)),
        ],
        compiler_params=params(48),
        cost_estimate=cost(3),
        name="panels",
    )(meta, rows_all, C0, M0h, M0l, C1, M1h, M1l, X1h, X1l)
    tiles = pl.BlockSpec((KIDS, 1, COLS, N, RK), lambda r: (0, r, 0, 0, 0))
    out = pl.pallas_call(
        final_kernel,
        grid=(ROWS,),
        out_shape=shape((ROWS, N, COLS * 4, 128), F32),
        in_specs=[
            SMEM,
            SMEM,
            VMEM,
            tiles,
            tiles,
            pl.BlockSpec((1, N, 2 * N), lambda r: (r, 0, 0)),
            pl.BlockSpec((1, N, N), lambda r: (r, 0, 0)),
        ]
        + [VMEM] * 2
        + [whole] * 6,
        out_specs=pl.BlockSpec((1, N, COLS * 4, 128), lambda r: (r, 0, 0, 0)),
        scratch_shapes=[
            pltpu.VMEM((COLS, N, 2 * N), BF16),
            pltpu.VMEM((PACK, 128), F32),
            pltpu.VMEM((N, N), F32),
        ],
        compiler_params=params(60),
        cost_estimate=cost(20),
        name="update",
    )(rank, meta, diag_shift, u, v, gb, panels, cols_all, kall,
      M0h, M0l, M1h, M1l, X1h, X1l)
    block = pl.BlockSpec(
        (1, N, COLS * 4, 128), lambda t, meta: (2 * t + meta[1] // PROW, 0, 0, 0)
    )
    out = pl.pallas_call(
        diagonal_kernel,
        grid_spec=pltpu.PrefetchScalarGridSpec(
            num_scalar_prefetch=1,
            grid=(COLS,),
            in_specs=[VMEM, block],
            out_specs=block,
            scratch_shapes=[pltpu.VMEM((PACK, 128), F32), pltpu.VMEM((N, N), F32)],
        ),
        out_shape=shape((ROWS, N, COLS * 4, 128), F32),
        input_output_aliases={2: 0},
        compiler_params=params(32),
        cost_estimate=cost(4),
        name="diagonal",
    )(meta, rall, out)
    return out.reshape(ROWS, 1, N, COLS, 1, N)


def solution(mesh):
    placed = (
        P(None, None, "prow", None, "pcol", None, None),
        P(None, None, "prow", None, "pcol", None, None),
        P(None, None, "prow", None, "pcol"),
        P(),
    )
    return jax.shard_map(
        on_device,
        mesh=mesh,
        in_specs=placed,
        out_specs=P(None, "prow", None, None, "pcol", None),
        check_vma=False,
    )
```

```python
import functools
import jax
import jax.numpy as jnp
from jax import lax
from jax.experimental import pallas as pl
from jax.experimental.pallas import tpu as pltpu
from jax.sharding import PartitionSpec as P

F32 = jnp.float32
BF16 = jnp.bfloat16
PROW, PCOL = 8, 16
ROWS, COLS, KIDS = 5, 2, 2
N, RK = 512, 128
TRI = [(a, b) for a in range(4) for b in range(a + 1)]
PACK = 128 * len(TRI)
KSLAB = PACK // PROW
RSLAB = PACK // PCOL
VMEM = pl.BlockSpec(memory_space=pltpu.VMEM)
SMEM = pl.BlockSpec(memory_space=pltpu.SMEM)
EXACT = lax.Precision.HIGHEST


def shape(dims, dtype):
    return jax.ShapeDtypeStruct(dims, dtype)


def cost(us):
    return pl.CostEstimate(flops=us * 1_000_000_000, transcendentals=0, bytes_accessed=1 << 20)


def params(mib):
    return pltpu.CompilerParams(vmem_limit_bytes=mib << 20)


def nt(a, b, precision=None):
    return lax.dot_general(
        a, b, (((1,), (1,)), ((), ())), precision=precision, preferred_element_type=F32
    )


def nn(a, b, precision=None):
    return lax.dot_general(
        a, b, (((1,), (0,)), ((), ())), precision=precision, preferred_element_type=F32
    )


def halves(x):
    hi = x.astype(BF16)
    return hi, (x - hi.astype(F32)).astype(BF16)


def kept(tile, rank):
    lane = lax.broadcasted_iota(jnp.int32, tile.shape, 1)
    return jnp.where(lane < rank, tile, jnp.zeros_like(tile))


def column_kernel(rank, v, out, cat, packed):
    for t in range(COLS):
        for c in range(KIDS):
            for r in range(ROWS):
                at = (c * ROWS + r) * RK
                cat[:, at : at + RK] = kept(v[c, r, t], rank[c, r, t])
        total = nt(cat[...], cat[...])
        for n, (a, b) in enumerate(TRI):
            packed[128 * n : 128 * n + 128, :] = total[
                128 * a : 128 * a + 128, 128 * b : 128 * b + 128
            ]
        for s in range(PROW):
            out[s, t] = packed[KSLAB * s : KSLAB * s + KSLAB, :]


def pieces_kernel(rank, meta, u, v, _, *refs):
    raw, tile, cols, masked = refs[:4], refs[4], refs[5:9], refs[9]
    root = jnp.where(meta[1] == 1, 1, 0)
    for c in range(KIDS):
        for r in range(ROWS):
            masked[c * ROWS + r] = kept(u[c, r, 0], rank[c, r, 0])
            masked[(KIDS + c) * ROWS + r] = kept(v[c, r, 0], rank[c, r, 0])
    for s in range(16):
        raw[s // 4][s % 4] = masked[:, 32 * s : 32 * s + 32, :]
    for s in range(8):
        part = slice(64 * s, 64 * s + 64)
        for a in range(2 * KIDS):
            tile[s // 4, a, 64 * (s % 4) : 64 * (s % 4) + 64, :] = masked[a * ROWS, part, :]
            for h in range(2):
                row = lax.rem(root + h, 2)
                to = cols[2 * h + s // 4]
                to[s % 4, a] = masked[a * ROWS + row, part, :]
                to[s % 4, 4 + a] = masked[a * ROWS + 2 + row, part, :]


def row_kernel(rank, u, _, rsum, cat):
    for r in range(4):
        for c in range(KIDS):
            for t in range(COLS):
                at = (2 * c + t) * RK
                cat[:, at : at + RK] = kept(u[c, r, t], rank[c, r, t])
        total = nt(cat[...], cat[...])
        for n, (a, b) in enumerate(TRI):
            for e in range(128 // 16):
                line = 128 * n + 16 * e
                rsum[line // RSLAB, r, line % RSLAB : line % RSLAB + 16, :] = total[
                    128 * a + 16 * e : 128 * a + 16 * e + 16, 128 * b : 128 * b + 128
                ]


def base_inverse(block):
    lane = lax.broadcasted_iota(jnp.int32, (8, 128), 1)
    sub = lax.broadcasted_iota(jnp.int32, (8, 128), 0)
    rows = [block[8 * v : 8 * v + 8, :] for v in range(16)]

    def wide(x):
        return jnp.broadcast_to(x, (8, 128))

    for J in range(16):
        inside = (lane >= 8 * J) & (lane < 8 * J + 8)
        B = [wide(rows[J][:, 8 * J + n : 8 * J + n + 1]) for n in range(8)]
        fwd = jnp.where(inside, jnp.where(lane - 8 * J == sub, 1.0, 0.0), rows[J])
        full = fwd
        roots = jnp.zeros((8, 128), F32)
        for k in range(8):
            r = lax.rsqrt(wide(B[k][k : k + 1, :]))
            row = wide(full[k : k + 1, :])
            mult = jnp.where(sub == k, 0.0, B[k] * (r * r))
            full = full - mult * row
            fwd = fwd - jnp.where(sub > k, mult, 0.0) * row
            for n in range(k + 1, 8):
                B[n] = B[n] - mult * wide(B[n][k : k + 1, :])
            roots = jnp.where(sub == k, r, roots)
        rows[J] = fwd * roots
        scaled = full * (roots * roots)
        Y = [wide(scaled[n : n + 1, :]) for n in range(8)]
        for v in range(J + 1, 16):
            b = [wide(rows[v][:, 8 * J + n : 8 * J + n + 1]) * Y[n] for n in range(8)]
            t = ((b[0] + b[1]) + (b[2] + b[3])) + ((b[4] + b[5]) + (b[6] + b[7]))
            rows[v] = jnp.where(inside, 0.0, rows[v]) - t
    return jnp.concatenate(
        [jnp.where(lane <= sub + 8 * v, rows[v], 0.0) for v in range(16)], axis=0
    )


def factor(A, C, M, steps):
    i = lax.broadcasted_iota(jnp.int32, (128, 128), 0)
    j = lax.broadcasted_iota(jnp.int32, (128, 128), 1)
    if steps[0] == 0:
        M[...] = jnp.zeros_like(M)
        C[...] = jnp.zeros_like(C)
    for b in steps:
        at = slice(128 * b, 128 * b + 128)
        inv = base_inverse(A[at, at])
        if b:
            left = nn(C[at, 0 : 128 * b], M[0 : 128 * b, 0 : 128 * b], EXACT)
            M[at, 0 : 128 * b] = -nn(inv, left, EXACT)
        M[at, at] = inv
        C[at, at] = jnp.where(i >= j, nt(A[at, at], inv, EXACT), 0.0)
        if b < 3:
            below = slice(128 * b + 128, N)
            panel = nt(A[below, at], inv, EXACT)
            C[below, at] = panel
            A[below, below] = A[below, below] - nt(panel, panel, EXACT)


def add_shift(A, line):
    i = lax.broadcasted_iota(jnp.int32, (N, N), 0)
    j = lax.broadcasted_iota(jnp.int32, (N, N), 1)
    A[...] = A[...] + jnp.where(i == j, line, 0.0)


def unpack(A, packed, mirror):
    for n, (a, b) in enumerate(TRI):
        block = packed[128 * n : 128 * n + 128, :]
        A[128 * a : 128 * a + 128, 128 * b : 128 * b + 128] = block
        if a != b:
            A[128 * b : 128 * b + 128, 128 * a : 128 * a + 128] = (
                block.T if mirror else jnp.zeros_like(block)
            )


def half_kernel(meta, own, other, shift, A, C, M, K1, packed):
    x, core = meta[2], meta[3]
    for s in range(4):
        chip = lax.rem(x - s + 4, 4)
        for part, lane in ((own, core), (other, 1 - core)):
            place = 2 * chip + lane
            at = pl.ds(pl.multiple_of(place * KSLAB, 8), KSLAB)
            packed[at, :] = part[s, 0:KSLAB, :]
            K1[at, :] = part[s, KSLAB : 2 * KSLAB, :]
    unpack(A, packed, False)
    add_shift(A, shift[0:1, :])
    factor(A, C, M, (0, 1))


def first_kernel(
    meta, A0, C0, M0, K1, town, tother, shift, C, Mh, Ml, Gb, A1, A, M, tile
):
    core = meta[3]
    for part, lane in ((town, core), (tother, 1 - core)):
        line = pl.multiple_of(lane * 256, 16)
        for a in range(4):
            tile[a, pl.ds(line, 256), :] = part[a]
    A[...] = A0[...]
    C[...] = C0[...]
    M[...] = M0[...]
    factor(A, C, M, (2, 3))
    hi, lo = halves(M[...])
    Mh[...] = hi
    Ml[...] = lo
    U = jnp.concatenate([tile[0], tile[1]], axis=1)
    V = jnp.concatenate([tile[2], tile[3]], axis=1)
    wh, wl = halves(nn(hi, V) + nn(lo, V))
    G = (nt(U, wh) + nt(U, wl)).astype(BF16)
    Gb[...] = G
    unpack(A, K1, False)
    add_shift(A, shift[1:2, :])
    A1[...] = A[...] + (nt(U, U) - nt(G, G))


def second_kernel(A1, Gb, C, Mh, Ml, Xh, Xl, A, M):
    A[...] = A1[...]
    factor(A, C, M, (0, 1, 2, 3))
    hi, lo = halves(M[...])
    Mh[...] = hi
    Ml[...] = lo
    xh, xl = halves(nn(hi, Gb[...]) + nn(lo, Gb[...]))
    Xh[...] = xh
    Xl[...] = xl


def solve(i, tiles, M0h, M0l, M1h, M1l, X1h, X1l):
    U0, V0, U1, V1 = tiles
    inverse = jnp.concatenate([M0h[...], M0l[...]], axis=1)
    wh, wl = halves(nn(inverse, jnp.concatenate([V0, V0], axis=0)))
    left = jnp.concatenate([U0, U0], axis=1)
    G0 = jnp.where(i > 0, nt(left, jnp.concatenate([wh, wl], axis=1)), 0.0)
    b0 = G0.astype(BF16)
    inverse = jnp.concatenate([M1h[...], M1l[...]], axis=1)
    wh, wl = halves(nn(inverse, jnp.concatenate([V1, V1], axis=0)))
    left = jnp.concatenate([U1, U1, -b0, -b0], axis=1)
    G1 = nt(left, jnp.concatenate([wh, wl, X1h[...], X1l[...]], axis=1))
    G1 = jnp.where(i > 1, G1, 0.0)
    return G0, G1, b0, G1.astype(BF16)


def pair(get, first):
    return jnp.concatenate([get(first), get(first + 1)], axis=1)


def panel_kernel(meta, rb, C0, M0h, M0l, C1, M1h, M1l, X1h, X1l, gb, side):
    r = pl.program_id(0)
    p, q = meta[0], meta[1]
    i = r * PROW + p
    tiles = []
    for k in range(2):
        def get(a, k=k):
            whole = rb[:, k, a * ROWS + r]
            if k:
                order = [4 * zz + yy for zz in range(4) for yy in (1, 2, 3, 0)]
                whole = jnp.concatenate([whole[e : e + 1] for e in order], axis=0)
            return whole.reshape(N, RK)
        tiles += [pair(get, 0), pair(get, 2)]
    G0, G1, b0, b1 = solve(i, tiles, M0h, M0l, M1h, M1l, X1h, X1l)
    gb[0, :, 0:N] = b0
    gb[0, :, N : 2 * N] = b1

    def panel(k, C, G):
        a = lax.broadcasted_iota(jnp.int32, (N, N), 0)
        b = lax.broadcasted_iota(jnp.int32, (N, N), 1)
        pivots = jnp.sum(jnp.where(a == b, C[...], 0.0), axis=0, keepdims=True)

        @pl.when(i == k)
        def _():
            side[0] = C[...] * pivots

        @pl.when(i != k)
        def _():
            side[0] = G * pivots

    @pl.when(q == 0)
    def _():
        panel(0, C0, G0)

    @pl.when(q == 1)
    def _():
        panel(1, C1, G1)

    @pl.when(q > 1)
    def _():
        side[...] = jnp.zeros_like(side)


def final_kernel(
    rank, meta, shift, u, v, gb, side, rc, ksum,
    M0h, M0l, M1h, M1l, X1h, X1l, out, gcol, packed, D
):
    r = pl.program_id(0)
    p, q = meta[0], meta[1]
    home = lax.rem(q, PROW)

    @pl.when(r == 0)
    def _():
        for t in range(COLS):
            tiles = []
            for k in range(2):
                def get(a, k=k, t=t):
                    return jnp.concatenate(
                        [
                            rc[
                                2 * lax.rem(home // 2 + s, 4) + lax.rem(home + c, 2),
                                k,
                                4 * t + a,
                            ]
                            for c in range(2)
                            for s in range(4)
                        ],
                        axis=0,
                    )
                tiles += [pair(get, 0), pair(get, 2)]
            _, _, b0, b1 = solve(q + PCOL * t, tiles, M0h, M0l, M1h, M1l, X1h, X1l)
            gcol[t, :, 0:N] = b0
            gcol[t, :, N : 2 * N] = b1

    i = r * PROW + p

    def put(t, value):
        for b in range(4):
            out[0, :, 4 * t + b, :] = value[:, 128 * b : 128 * b + 128]

    def trailing(t):
        j = q + PCOL * t
        U = jnp.concatenate([u[c, 0, t] for c in range(KIDS)], axis=1)
        V = jnp.concatenate([kept(v[c, 0, t], rank[c, r, t]) for c in range(KIDS)], axis=1)
        acc = nt(U, V) - nt(gb[0], gcol[t])
        put(t, jnp.where(i >= j, acc, 0.0))

        @pl.when(i == j)
        def _():
            for e in range(PROW):
                packed[KSLAB * e : KSLAB * e + KSLAB, :] = ksum[e, t]
            unpack(D, packed, True)
            add_shift(D, shift[pl.ds(j, 1), :])
            put(t, acc + D[...])

    @pl.when(q > 1)
    def _():
        trailing(0)

    @pl.when(q <= 1)
    def _():
        put(0, side[0])

    trailing(1)


def diagonal_kernel(meta, rsum, old, out, packed, D):
    t = pl.program_id(0)
    out[...] = old[...]

    @pl.when((meta[0] == lax.rem(meta[1], PROW)) & (meta[1] + PCOL * t > 1))
    def _():
        for e in range(PCOL):
            packed[RSLAB * e : RSLAB * e + RSLAB, :] = rsum[e, t]
        unpack(D, packed, True)
        for k in range(COLS):
            @pl.when(t == k)
            def _():
                for b in range(4):
                    out[0, :, 4 * k + b, :] = (
                        out[0, :, 4 * k + b, :] + D[:, 128 * b : 128 * b + 128]
                    )


def total(values):
    return functools.reduce(lambda a, b: a + b, values)


def pick(flag, value):
    return jnp.where(flag, value, jnp.zeros_like(value))


def on_device(child_u, child_v, child_rank, diag_shift):
    p = lax.axis_index("prow")
    q = lax.axis_index("pcol")
    x, core = p // 2, p % 2
    z, y = q // 4, q % 4
    both = ("prow", "pcol")
    rank = child_rank[:, :, 0, :, 0]
    u = child_u[:, :, 0, :, 0]
    v = child_v[:, :, 0, :, 0]
    meta = jnp.stack([p, q, x, core]).astype(jnp.int32)

    sums = pl.pallas_call(
        column_kernel,
        out_shape=shape((PROW, COLS, KSLAB, 128), F32),
        in_specs=[SMEM, VMEM],
        out_specs=VMEM,
        scratch_shapes=[
            pltpu.VMEM((N, KIDS * ROWS * RK), BF16),
            pltpu.VMEM((PACK, 128), F32),
        ],
        compiler_params=params(32),
        cost_estimate=cost(3),
        name="column_sums",
    )(rank, v)
    parts = pl.pallas_call(
        pieces_kernel,
        out_shape=[shape((4, 4 * ROWS, 32, RK), BF16)] * 4
        + [shape((2, 4, 256, RK), BF16)]
        + [shape((4, 8, 64, RK), BF16)] * 4,
        in_specs=[SMEM, SMEM, VMEM, VMEM, pl.BlockSpec(memory_space=pl.ANY)],
        out_specs=[VMEM] * 9,
        scratch_shapes=[pltpu.VMEM((4 * ROWS, N, RK), BF16)],
        compiler_params=params(48),
        cost_estimate=cost(4),
        name="pieces",
    )(rank, meta, u, v, sums)
    raw, tile, cols = parts[:4], parts[4], parts[5:9]
    swap = [(i, i ^ 1) for i in range(8)]
    turn = [
        [(2 * a + c, 2 * ((a + s) % 4) + c) for a in range(4) for c in range(2)]
        for s in range(1, 4)
    ]
    down = [[(i, 4 * s + i) for i in range(4)] for s in range(1, 4)]

    kgot = lax.all_to_all(sums, "prow", 0, 0)
    tgot = [lax.ppermute(tile, both, [(PCOL, PCOL + s)]) for s in range(1, 4)]
    zgot = [lax.ppermute(raw[s], "pcol", [(k, 4 * s + k) for k in range(2)]) for s in range(1, 4)]
    kgot, tgot, zgot = lax.optimization_barrier((kgot, tgot, zgot))
    kslab = jnp.sum(kgot, axis=0)
    kall = lax.all_gather(kslab, "prow")

    got = [lax.ppermute(kslab[0], "pcol", [(0, s), (1, (1 + s) % 4)]) for s in range(1, 4)]
    tpay = pick((p == 1) & (q == 0), tile) + total(tgot)
    tgot = [
        lax.ppermute(tpay, both, [(PCOL + i, PCOL + 4 * s + i) for i in range(4)])
        for s in range(1, 4)
    ]
    got, tgot = lax.optimization_barrier((got, tgot))
    pay = [
        pick(y == k, kslab[0]) + total(pick((y + 4 - k) % 4 == s, got[s - 1]) for s in range(1, 4))
        for k in range(2)
    ]
    pay = pick(z == 0, jnp.concatenate(pay, axis=0))
    tpay = pick(z == 0, tpay) + total(tgot)

    got = [lax.ppermute(pay, "pcol", pairs) for pairs in down]
    thalf = lax.ppermute(tpay[0], "prow", [(1, 0)])
    hold = [
        pick(z == 0, raw[0][s]) + total(zgot[e][s] for e in range(3)) for s in range(4)
    ]
    ygot = [
        lax.ppermute(
            hold[s], "pcol", [(4 * a + k, 4 * a + (k + s) % 4) for a in range(4) for k in range(2)]
        )
        for s in range(1, 4)
    ]
    got, ygot, thalf, kall = lax.optimization_barrier((got, ygot, thalf, kall))
    pay = pay + total(got)
    thalf = jnp.where(core == 1, tpay[1], thalf)
    piece = jnp.stack(
        [
            pick(y == k, hold[0]) + total(pick((y + 4 - k) % 4 == s, ygot[s - 1]) for s in range(1, 4))
            for k in range(2)
        ]
    )
    rows_all = lax.all_gather(piece, "pcol")

    got = [lax.ppermute(pay, "prow", pairs) for pairs in turn]
    tgot = [
        lax.ppermute(thalf, "prow", [(c, 2 * s + c) for c in range(2)]) for s in range(1, 4)
    ]
    rsum = pl.pallas_call(
        row_kernel,
        out_shape=shape((PCOL, 4, RSLAB, 128), F32),
        in_specs=[SMEM, VMEM, pl.BlockSpec(memory_space=pl.ANY)],
        out_specs=VMEM,
        scratch_shapes=[pltpu.VMEM((N, 4 * RK), BF16)],
        compiler_params=params(32),
        cost_estimate=cost(4),
        name="row_sums",
    )(rank, u, kslab)
    got, tgot, rsum, cols, piece = lax.optimization_barrier((got, tgot, rsum, cols, piece))
    thalf = pick(x == 0, thalf) + total(tgot)
    tother = lax.ppermute(thalf, "prow", swap)

    own = jnp.stack([pay] + got)
    other = lax.ppermute(own, "prow", swap)
    arrived = [
        lax.ppermute(
            cols[2 * h + c],
            both,
            [
                (a * PCOL + k, (a ^ c) * PCOL + a + 8 * (h ^ k))
                for a in range(8)
                for k in range(2)
            ],
        )
        for h in range(2)
        for c in range(2)
    ]
    own, other, tother = lax.optimization_barrier((own, other, tother))

    square = shape((N, N), F32)
    narrow = shape((N, N), BF16)
    work = pltpu.VMEM((N, N), F32)
    A0, C0, M0, K1 = pl.pallas_call(
        half_kernel,
        out_shape=[square] * 3 + [shape((PACK, 128), F32)],
        in_specs=[SMEM] + [VMEM] * 3,
        out_specs=[VMEM] * 4,
        scratch_shapes=[pltpu.VMEM((PACK, 128), F32)],
        compiler_params=params(32),
        cost_estimate=cost(14),
        name="first_pivot_a",
    )(meta, own, other, diag_shift)
    C0, M0h, M0l, g01, A1 = pl.pallas_call(
        first_kernel,
        out_shape=[square, narrow, narrow, narrow, square],
        in_specs=[SMEM] + [VMEM] * 7,
        out_specs=[VMEM] * 5,
        scratch_shapes=[work, work, pltpu.VMEM((4, N, RK), BF16)],
        compiler_params=params(32),
        cost_estimate=cost(15),
        name="first_pivot_b",
    )(meta, A0, C0, M0, K1, thalf, tother, diag_shift)
    arrived, rsum, A1 = lax.optimization_barrier((arrived, rsum, A1))
    rparts = lax.all_to_all(rsum, "pcol", 0, 0)
    side = q // 8
    arrived = [arrived[0] + arrived[1], arrived[2] + arrived[3]]
    hold = jnp.stack(
        [jnp.where(side == 0, arrived[k], arrived[1 - k]) for k in range(2)], axis=1
    )
    lines = [
        [
            (a * PCOL + b, (a + 2 * s) % 8 * PCOL + b)
            for b in range(PCOL)
            for a in (b % 8 // 2 * 2, b % 8 // 2 * 2 + 1)
        ]
        for s in range(1, 4)
    ]
    sent = [lax.ppermute(hold[s], both, lines[s - 1]) for s in range(1, 4)]
    A1, hold = lax.optimization_barrier((A1, hold))
    C1, M1h, M1l, X1h, X1l = pl.pallas_call(
        second_kernel,
        out_shape=[square] + [narrow] * 4,
        in_specs=[VMEM] * 2,
        out_specs=[VMEM] * 5,
        scratch_shapes=[work, work],
        compiler_params=params(32),
        cost_estimate=cost(26),
        name="second_pivot",
    )(A1, g01)
    sent, rows_all, rparts, C1 = lax.optimization_barrier((sent, rows_all, rparts, C1))
    share = pick(x == (q % 8) // 2, hold[0]) + total(sent)
    cols_all = lax.all_gather(share, "prow")
    C1, share = lax.optimization_barrier((C1, share))
    rown = jnp.sum(rparts, axis=0)
    rown = jnp.concatenate(
        [
            jnp.broadcast_to(jnp.stack([rown[h], rown[2 + h]]), (8, COLS, RSLAB, 128))
            for h in range(2)
        ],
        axis=0,
    )
    rall = lax.all_to_all(rown, "pcol", 0, 0)
    C1, rown = lax.optimization_barrier((C1, rown))
    whole = pl.BlockSpec((N, N), lambda r: (0, 0))
    gb, panels = pl.pallas_call(
        panel_kernel,
        grid=(ROWS,),
        out_shape=[shape((ROWS, N, 2 * N), BF16), shape((ROWS, N, N), F32)],
        in_specs=[SMEM, VMEM] + [whole] * 8,
        out_specs=[
            pl.BlockSpec((1, N, 2 * N), lambda r: (r, 0, 0)),
            pl.BlockSpec((1, N, N), lambda r: (r, 0, 0)),
        ],
        compiler_params=params(48),
        cost_estimate=cost(3),
        name="panels",
    )(meta, rows_all, C0, M0h, M0l, C1, M1h, M1l, X1h, X1l)
    tiles = pl.BlockSpec((KIDS, 1, COLS, N, RK), lambda r: (0, r, 0, 0, 0))
    out = pl.pallas_call(
        final_kernel,
        grid=(ROWS,),
        out_shape=shape((ROWS, N, COLS * 4, 128), F32),
        in_specs=[
            SMEM,
            SMEM,
            VMEM,
            tiles,
            tiles,
            pl.BlockSpec((1, N, 2 * N), lambda r: (r, 0, 0)),
            pl.BlockSpec((1, N, N), lambda r: (r, 0, 0)),
        ]
        + [VMEM] * 2
        + [whole] * 6,
        out_specs=pl.BlockSpec((1, N, COLS * 4, 128), lambda r: (r, 0, 0, 0)),
        scratch_shapes=[
            pltpu.VMEM((COLS, N, 2 * N), BF16),
            pltpu.VMEM((PACK, 128), F32),
            pltpu.VMEM((N, N), F32),
        ],
        compiler_params=params(60),
        cost_estimate=cost(20),
        name="update",
    )(rank, meta, diag_shift, u, v, gb, panels, cols_all, kall,
      M0h, M0l, M1h, M1l, X1h, X1l)
    block = pl.BlockSpec(
        (1, N, COLS * 4, 128), lambda t, meta: (2 * t + meta[1] // PROW, 0, 0, 0)
    )
    out = pl.pallas_call(
        diagonal_kernel,
        grid_spec=pltpu.PrefetchScalarGridSpec(
            num_scalar_prefetch=1,
            grid=(COLS,),
            in_specs=[VMEM, block],
            out_specs=block,
            scratch_shapes=[pltpu.VMEM((PACK, 128), F32), pltpu.VMEM((N, N), F32)],
        ),
        out_shape=shape((ROWS, N, COLS * 4, 128), F32),
        input_output_aliases={2: 0},
        compiler_params=params(32),
        cost_estimate=cost(4),
        name="diagonal",
    )(meta, rall, out)
    return out.reshape(ROWS, 1, N, COLS, 1, N)


def solution(mesh):
    placed = (
        P(None, None, "prow", None, "pcol", None, None),
        P(None, None, "prow", None, "pcol", None, None),
        P(None, None, "prow", None, "pcol"),
        P(),
    )
    return jax.shard_map(
        on_device,
        mesh=mesh,
        in_specs=placed,
        out_specs=P(None, "prow", None, None, "pcol", None),
        check_vma=False,
    )
```
